128 devices in a mesh: row: 16 (over y, z), col: 8 (over x, core).
Axes of the slice: x: 4, y: 4, z: 4, core: 2. Of those that a mesh axis runs over, the one named last changes fastest.
Arguments:
- glob_derivs: bfloat16 [128, 16, 256, 128], P(('row', 'col')), may hold values from -0.09375 to 0.09375
- local_derivs: float32 [128, 16, 4, 256], P(('row', 'col')), may hold values from -6 to 6
- weights: float32 [128, 16, 256], P(('row', 'col')), may hold values from 0.25 to 4
- residuals: float32 [128, 16, 256], P(('row', 'col')), may hold values from -6 to 6
- track_ids: int32 [128, 16, 256], P(('row', 'col')), may hold values from 0 to 255
- module_blocks: int32 [128, 16], replicated, may hold values from 0 to 7
- weak_modes: float32 [16384, 64], P('col'), may hold values from -6 to 6
Outputs:
- schur: float32 [16384, 16384], P('row', 'col')
- layer_blocks: float32 [16384, 1024], P('row', 'col')
- rhs: float32 [16384], P('row')
- weak_product: float32 [16384, 64], P(('row', 'col'))
The draws below stay inside these ranges and needn't reach their ends.
All inputs are finite; a program needn't handle non-finite values.
Results may differ from the reference program's by a relative error of at most 0.0094.
Values sent between devices are 32-bit elements; how exact they have to be, the bound alone decides.
A program may use at most 128 MiB of HBM per device.

```python
import math
import jax
import jax.numpy as jnp
from jax import lax

BW = 128
GB = 8
LOC = 4
TRK = 256
PER = 256
MODES = 64
LAYERS = 16
BUNDLES = 128
ORDER = 16384


def set_ends(drawn, own_key, least, largest):
    index_at = [jax.random.randint(jax.random.fold_in(own_key, axis), (), 0, length) for axis, length in enumerate(drawn.shape)]
    longest = drawn.shape.index(max(drawn.shape))
    neighbour = index_at[:longest] + [(index_at[longest] + 1) % drawn.shape[longest]] + index_at[longest + 1:]
    return drawn.at[tuple(index_at)].set(least).at[tuple(neighbour)].set(largest)


def steps_of(key, extent, shards, low, top_value):
    gain = 1.0
    for position, blocks in shards:
        steps = jax.random.uniform(jax.random.fold_in(jax.random.fold_in(key, 6), position), (blocks,), jnp.float32, low / len(shards), top_value / len(shards))
        gain = gain * jnp.repeat(jnp.exp(steps), extent[position] // blocks).reshape((-1,) + (1,) * (len(extent) - 1 - position))
    return gain


def bell_draw(stream_key, shape, width, most, pieces=(), held_as=jnp.bfloat16):
    entries = width * jax.random.normal(stream_key, shape, jnp.float32)
    if pieces:
        entries = entries * steps_of(stream_key, shape, pieces, -0.22, 0.18)
    return jnp.clip(entries, -most, most).astype(held_as)


def setup_inputs(seed: int = 0) -> dict:
    key_of = jax.random.split(jax.random.key(seed), 8)
    return {
        "glob_derivs": bell_draw(key_of[0], (BUNDLES, LAYERS, PER, BW), (PER * BUNDLES // GB) ** -0.5, 0.09375, ((0, 128),)),
        "local_derivs": bell_draw(key_of[1], (BUNDLES, LAYERS, LOC, PER), 1.0, 6.0, ((0, 128),), jnp.float32),
        "weights": jnp.clip(jnp.exp(math.log(4.0) - 2.7725887 * jax.random.uniform(key_of[2], (BUNDLES, LAYERS, PER), jnp.float32) ** steps_of(key_of[2], (BUNDLES, LAYERS, PER), ((0, 128),), -0.2, 0.2)), 0.25, 4.0),
        "residuals": bell_draw(key_of[3], (BUNDLES, LAYERS, PER), 1.0, 6.0, ((0, 128),), jnp.float32),
        "track_ids": set_ends(jax.random.randint(key_of[4], (BUNDLES, LAYERS, PER), 0, TRK), jax.random.fold_in(key_of[4], 1), 0, TRK - 1).astype(jnp.int32),
        "module_blocks": set_ends(jax.random.randint(key_of[5], (BUNDLES, LAYERS), 0, GB), jax.random.fold_in(key_of[5], 1), 0, GB - 1).astype(jnp.int32),
        "weak_modes": bell_draw(key_of[6], (ORDER, MODES), 1.0, 6.0, ((0, 8),), jnp.float32),
    }


def invert(matrix):
    count = matrix.shape[0]
    rows = [matrix[i] for i in range(count)]
    inverse = [jnp.zeros_like(matrix[0]).at[i].set(1.0) for i in range(count)]
    for pivot_row in range(count):
        pivot = rows[pivot_row][pivot_row]
        scaled = rows[pivot_row] / pivot
        scaled_inv = inverse[pivot_row] / pivot
        for other in range(count):
            if other != pivot_row:
                factor = rows[other][pivot_row]
                rows[other] = rows[other] - factor * scaled
                inverse[other] = inverse[other] - factor * scaled_inv
        rows[pivot_row] = scaled
        inverse[pivot_row] = scaled_inv
    return jnp.stack(inverse)


def bundle_terms(glob, local, weight, resid, tracks):
    layers = glob.shape[0]
    f32 = jnp.float32
    onehot = (tracks[:, :, None] == jnp.arange(TRK)[None, None, :]).astype(f32)
    weighted = weight[:, None, :] * local
    spread = onehot[:, :, :, None] * jnp.transpose(weighted, (0, 2, 1))[:, :, None, :]
    u_rows = spread.reshape(layers, glob.shape[1], TRK * LOC).astype(jnp.bfloat16)
    h_mat = jnp.einsum('spi,spk->sik', glob.astype(f32), u_rows.astype(f32)).astype(jnp.bfloat16)
    prods = weighted[:, :, None, :] * local[:, None, :, :]
    normal = jnp.einsum('sijm,smt->ijt', prods, onehot, precision=lax.Precision.HIGHEST)
    normal = normal + jnp.eye(LOC, dtype=f32)[:, :, None]
    qvec = jnp.einsum('sjm,smt->jt', weighted * resid[:, None, :], onehot, precision=lax.Precision.HIGHEST)
    kinv = invert(normal)
    h_wide = h_mat.astype(f32).reshape(layers, BW, TRK, LOC)
    x_wide = jnp.zeros_like(h_wide)
    for lidx in range(LOC):
        x_wide = x_wide + h_wide[..., lidx:lidx + 1] * jnp.transpose(kinv[lidx])[None, None]
    x_mat = x_wide.reshape(layers, BW, TRK * LOC).astype(jnp.bfloat16)
    wglob = (weight[:, :, None] * glob.astype(f32)).astype(jnp.bfloat16)
    diag_tiles = jnp.einsum('spi,spj->sij', wglob.astype(f32), glob.astype(f32))
    wres = (weight * resid).astype(jnp.bfloat16)
    qflat = jnp.transpose(qvec).reshape(TRK * LOC).astype(jnp.bfloat16)
    vec = jnp.einsum('sp,spi->si', wres.astype(f32), glob.astype(f32)) - jnp.einsum('sik,k->si', x_mat.astype(f32), qflat.astype(f32))
    gram = jnp.einsum('rip,ljp->rlij', x_mat.astype(f32), h_mat.astype(f32))
    tiles = jnp.eye(layers, dtype=f32)[:, :, None, None] * diag_tiles[:, None, :, :] - gram
    return tiles, vec


def reference(glob_derivs, local_derivs, weights, residuals, track_ids, module_blocks, weak_modes):
    def step(carry, items):
        matrix, vector = carry
        glob, local, weight, resid, tracks, blocks = items
        tiles, vec = bundle_terms(glob, local, weight, resid, tracks)
        base = (jnp.arange(LAYERS).astype(jnp.int32) * (GB * BW) + blocks.astype(jnp.int32) * BW)
        index = (base[:, None] + jnp.arange(BW).astype(jnp.int32)[None, :]).reshape(-1).astype(jnp.int32)
        square = jnp.transpose(tiles, (0, 2, 1, 3)).reshape(LAYERS * BW, LAYERS * BW)
        matrix = matrix.at[index[:, None], index[None, :]].add(square)
        vector = vector.at[index].add(vec.reshape(-1))
        return (matrix, vector), None

    start = (jnp.zeros((ORDER, ORDER), jnp.float32), jnp.zeros((ORDER,), jnp.float32))
    (full, rhs), _ = lax.scan(step, start, (glob_derivs, local_derivs, weights, residuals, track_ids, module_blocks))
    weak_product = jnp.dot(full, weak_modes, precision=lax.Precision.HIGHEST, preferred_element_type=jnp.float32)
    span = GB * BW
    layer_blocks = jnp.concatenate([full[lidx * span:(lidx + 1) * span, lidx * span:(lidx + 1) * span] for lidx in range(LAYERS)], axis=0)
    layer_of = jnp.arange(ORDER).astype(jnp.int32) // span
    schur = jnp.where(layer_of[:, None] == layer_of[None, :], jnp.zeros((), full.dtype), full)
    return schur, layer_blocks, rhs, weak_product
```

```python
import functools

import jax
import jax.numpy as jnp
from jax import lax
from jax.experimental import pallas as pl
from jax.experimental.pallas import tpu as pltpu
from jax.sharding import PartitionSpec as P

BW = 128
GB = 8
LOC = 4
TRK = 256
LAYERS = 16
PER = 256
ROWS = 88
SIZE = {"y": 4, "z": 4, "X": 8}
ORDERS = (("y", "z", "X"), ("z", "X", "y"), ("X", "y", "z"))
RING = (1, 3, 2)
WIDE = (2, 3, 6, 7, 1, 4, 5)
MESH = pl.DeviceIdType.MESH
f32 = jnp.float32
bf16 = jnp.bfloat16


def split3(v):
    hi = v.astype(bf16)
    rest = v - hi.astype(f32)
    mid = rest.astype(bf16)
    low = (rest - mid.astype(f32)).astype(bf16)
    return hi, mid, low


def nt(a, b):
    return lax.dot_general(a, b, (((1,), (1,)), ((), ())), preferred_element_type=f32)


def nn(a, b):
    return lax.dot_general(a, b, (((1,), (0,)), ((), ())), preferred_element_type=f32)


def head_kernel(
    glob, local, weight, resid, tracks, a0, a1, a2, h_all, x_all, d_all, v_all, sums, q_ref, k_ref
):
    c = pl.program_id(0)

    @pl.when(c == 0)
    def _():
        sums[...] = jnp.zeros_like(sums)

        def first(s, carry):
            g = glob[s]
            gt = jnp.transpose(g.astype(f32))
            gt_low = gt.astype(bf16)
            t = tracks[pl.ds(s, 1), :]
            w = weight[pl.ds(s, 1), :]
            r = resid[pl.ds(s, 1), :]
            hot = lax.broadcasted_iota(jnp.int32, (TRK, PER), 0) == t
            a = local[s]
            wa = w * a
            zero = jnp.zeros((), f32)
            row = pl.ds(pl.multiple_of(s * BW, BW), BW)
            for j in range(LOC):
                spread = jnp.where(hot, wa[j : j + 1, :], zero).astype(bf16)
                h_all[row, j * TRK : (j + 1) * TRK] = nt(gt_low, spread).astype(bf16)
            terms = []
            for i in range(LOC):
                terms.append(wa[i : i + 1, :] * a)
            terms.append(wa * r)
            terms.append(jnp.zeros((4, PER), f32))
            stacked = jnp.concatenate(terms, axis=0)
            hot_low = jnp.where(hot, jnp.ones((), f32), zero).astype(bf16)
            hi, mid, low = split3(stacked)
            sums[...] += nt(hi, hot_low) + nt(mid, hot_low) + nt(low, hot_low)
            d_all[row, :] = nn((gt * w).astype(bf16), g)
            wr = jnp.broadcast_to((w * r).astype(bf16), (16, PER))
            v_all[pl.ds(pl.multiple_of(s * 8, 8), 8), :] = nn(wr, g)[:8]
            return carry

        lax.fori_loop(0, LAYERS, first, 0)

        one = jnp.ones((1, TRK), f32)
        nil = jnp.zeros((1, TRK), f32)
        rows = [
            [
                sums[4 * i + j : 4 * i + j + 1, :] + (one if i == j else nil)
                for j in range(LOC)
            ]
            for i in range(LOC)
        ]
        inv = [[one if i == j else nil for j in range(LOC)] for i in range(LOC)]
        for p in range(LOC):
            pivot = rows[p][p]
            scaled = [v / pivot for v in rows[p]]
            scaled_inv = [v / pivot for v in inv[p]]
            for o in range(LOC):
                if o != p:
                    factor = rows[o][p]
                    rows[o] = [u - factor * v for u, v in zip(rows[o], scaled)]
                    inv[o] = [u - factor * v for u, v in zip(inv[o], scaled_inv)]
            rows[p] = scaled
            inv[p] = scaled_inv
        for i in range(LOC):
            for j in range(LOC):
                k_ref[4 * i + j : 4 * i + j + 1, :] = inv[i][j]
        for j in range(LOC):
            q_ref[:, j * TRK : (j + 1) * TRK] = jnp.broadcast_to(
                sums[16 + j : 17 + j, :].astype(bf16), (16, TRK)
            )

        def second(s, carry):
            row = pl.ds(pl.multiple_of(s * BW, BW), BW)
            h = [h_all[row, l * TRK : (l + 1) * TRK].astype(f32) for l in range(LOC)]
            for j in range(LOC):
                x = h[0] * k_ref[j : j + 1, :]
                for l in range(1, LOC):
                    x = x + h[l] * k_ref[4 * l + j : 4 * l + j + 1, :]
                x_all[row, j * TRK : (j + 1) * TRK] = (-x).astype(bf16)
            v = pl.ds(pl.multiple_of(s * 8, 8), 8)
            v_all[v, :] = v_all[v, :] + nt(q_ref[...], x_all[row, :])[:8]
            return carry

        lax.fori_loop(0, LAYERS, second, 0)

    right = h_all[pl.ds(pl.multiple_of(c * 2 * BW, 2 * BW), 2 * BW), :]

    def gram(s2, carry):
        out = nt(x_all[pl.ds(pl.multiple_of(s2 * 4 * BW, 4 * BW), 4 * BW), :], right)
        for z in range(4):
            part = out[z * BW : (z + 1) * BW, :]
            a0[s2, z, 0] = part[0:88, :BW]
            a1[z, 0, s2, 0:40] = part[88:BW, :BW]
            a1[z, 0, s2, 40:88] = part[0:48, BW:]
            a2[0, s2, z, 0:80] = part[48:BW, BW:]
            a2[0, s2, z, 80:88] = v_all[pl.ds(pl.multiple_of((s2 * 4 + z) * 8, 8), 8), :]
        return carry

    lax.fori_loop(0, 4, gram, 0)
    s = 2 * c
    y, z = s // 4, s % 4
    base = pl.multiple_of(s * BW, BW)
    a0[y, z, 0] += d_all[pl.ds(base, 88), :]
    a1[z, 0, y, 0:40] += d_all[pl.ds(base + 88, 40), :]
    s = 2 * c + 1
    y, z = s // 4, s % 4
    base = pl.multiple_of(s * BW, BW)
    a1[z, 0, y, 40:88] += d_all[pl.ds(base, 48), :]
    a2[0, y, z, 0:80] += d_all[pl.ds(base + 48, 80), :]


def head(glob, local, weight, resid, tracks):
    def whole(*shape):
        return pl.BlockSpec(shape, lambda c: (0,) * len(shape))

    return pl.pallas_call(
        head_kernel,
        grid=(8,),
        in_specs=[
            whole(LAYERS, PER, BW),
            whole(LAYERS, LOC, PER),
            whole(LAYERS, PER),
            whole(LAYERS, PER),
            whole(LAYERS, PER),
        ],
        out_specs=(
            pl.BlockSpec((4, 4, 1, ROWS, BW), lambda c: (0, 0, c, 0, 0)),
            pl.BlockSpec((4, 1, 4, ROWS, BW), lambda c: (0, c, 0, 0, 0)),
            pl.BlockSpec((1, 4, 4, ROWS, BW), lambda c: (c, 0, 0, 0, 0)),
        ),
        out_shape=tuple(
            jax.ShapeDtypeStruct(tuple(SIZE[d] for d in order) + (ROWS, BW), f32)
            for order in ORDERS
        ),
        scratch_shapes=[
            pltpu.VMEM((LAYERS * BW, LOC * TRK), bf16),
            pltpu.VMEM((LAYERS * BW, LOC * TRK), bf16),
            pltpu.VMEM((LAYERS * BW, BW), f32),
            pltpu.VMEM((LAYERS * 8, BW), f32),
            pltpu.VMEM((24, TRK), f32),
            pltpu.VMEM((16, LOC * TRK), bf16),
            pltpu.VMEM((16, TRK), f32),
        ],
        compiler_params=pltpu.CompilerParams(
            dimension_semantics=("arbitrary",), vmem_limit_bytes=56 << 20
        ),
        name="head",
    )(glob, local, weight, resid, tracks)


def coords():
    r, c = lax.axis_index("row"), lax.axis_index("col")
    return {"y": r // 4, "z": r % 4, "X": c}


def moved(me, dim, offset, sign):
    if dim == "X":
        x, k = me["X"] // 2, me["X"] % 2
        dx, dk = offset // 2, offset % 2
        return ((x + 4 + sign * dx) % 4) * 2 + (k + dk) % 2
    return (me[dim] + 4 + sign * offset) % 4


def device(me, dim, place):
    at = dict(me)
    at[dim] = place
    return (at["y"] * 4 + at["z"], at["X"])


def offsets(dim):
    return WIDE if dim == "X" else RING


def exchange_kernel(a0, a1, a2, *refs):
    a = (a0, a1, a2)
    e, b, cc = refs[0:3], refs[3:6], refs[6:9]
    bounce2, bounce3 = refs[9:12], refs[12:15]
    s1, r1, s2, r2, s3, r3, lsem = refs[15:22]
    me = coords()
    sends = []
    locals_ = []

    def send(src, dst, ssem, rsem, dim, place):
        cp = pltpu.make_async_remote_copy(
            src_ref=src,
            dst_ref=dst,
            send_sem=ssem,
            recv_sem=rsem,
            device_id=device(me, dim, place),
            device_id_type=MESH,
        )
        cp.start()
        sends.append(cp)
        return cp

    def local(src, mid, dst, i):
        into = pltpu.make_async_copy(src, mid, lsem.at[i])
        into.start()
        into.wait()
        out = pltpu.make_async_copy(mid, dst, lsem.at[i])
        out.start()
        return out

    first = {}
    for step in range(7):
        for g, order in enumerate(ORDERS):
            d1 = order[0]
            offs = offsets(d1)
            if step < len(offs):
                o = offs[step]
                to = moved(me, d1, o, 1)
                first[g, o] = send(
                    a[g].at[to], b[g].at[me[d1]], s1.at[g, o], r1.at[g, o], d1, to
                )
    second = {}
    back2 = {}
    count = 0
    for step in range(8):
        for g, order in enumerate(ORDERS):
            d1, d2, _ = order
            offs = (0,) + offsets(d1)
            if step >= len(offs):
                continue
            o1 = offs[step]
            src1 = moved(me, d1, o1, -1)
            if o1:
                first[g, o1].wait_recv()
            for o2 in offsets(d2):
                to = moved(me, d2, o2, 1)
                src = b[g].at[src1, to] if o1 else a[g].at[me[d1], to]
                second[g, o1, o2] = send(
                    src, cc[g].at[me[d2], src1], s2.at[g, o1, o2], r2.at[g, o1, o2], d2, to
                )
            src = b[g].at[src1, me[d2]] if o1 else a[g].at[me[d1], me[d2]]
            back2[g, o1] = local(src, bounce2[g].at[o1], cc[g].at[me[d2], src1], count)
            count += 1
    third = []
    for step in range(8):
        for g, order in enumerate(ORDERS):
            d1, d2, d3 = order
            offs = (0,) + offsets(d2)
            if step >= len(offs):
                continue
            o2 = offs[step]
            src2 = moved(me, d2, o2, -1)
            for o1 in (0,) + offsets(d1):
                if o2:
                    second[g, o1, o2].wait_recv()
                else:
                    back2[g, o1].wait()
            for o3 in offsets(d3):
                to = moved(me, d3, o3, 1)
                third.append(
                    send(
                        cc[g].at[src2, :, to],
                        e[g].at[me[d3], src2],
                        s3.at[g, o2, o3],
                        r3.at[g, o2, o3],
                        d3,
                        to,
                    )
                )
            locals_.append(
                local(cc[g].at[src2, :, me[d3]], bounce3[g].at[o2], e[g].at[me[d3], src2], count)
            )
            count += 1
    for cp in locals_:
        cp.wait()
    for cp in third:
        cp.wait_recv()
    for cp in sends:
        cp.wait_send()


def exchange(a0, a1, a2):
    item = (ROWS, BW)
    sizes = [tuple(SIZE[d] for d in order) for order in ORDERS]
    shapes = (
        [jax.ShapeDtypeStruct((n3, n2, n1) + item, f32) for n1, n2, n3 in sizes]
        + [jax.ShapeDtypeStruct((n1, n2, n3) + item, f32) for n1, n2, n3 in sizes]
        + [jax.ShapeDtypeStruct((n2, n1, n3) + item, f32) for n1, n2, n3 in sizes]
    )
    any_ = pl.BlockSpec(memory_space=pl.ANY)
    out = pl.pallas_call(
        exchange_kernel,
        out_shape=tuple(shapes),
        in_specs=[any_] * 3,
        out_specs=(any_,) * 9,
        scratch_shapes=[pltpu.VMEM((n1, n3) + item, f32) for n1, n2, n3 in sizes]
        + [pltpu.VMEM((n2, n1) + item, f32) for n1, n2, n3 in sizes]
        + [
            pltpu.SemaphoreType.DMA((3, 8)),
            pltpu.SemaphoreType.DMA((3, 8)),
            pltpu.SemaphoreType.DMA((3, 8, 8)),
            pltpu.SemaphoreType.DMA((3, 8, 8)),
            pltpu.SemaphoreType.DMA((3, 8, 8)),
            pltpu.SemaphoreType.DMA((3, 8, 8)),
            pltpu.SemaphoreType.DMA((32,)),
        ],
        compiler_params=pltpu.CompilerParams(
            has_side_effects=True, vmem_limit_bytes=56 << 20
        ),
        name="exchange",
    )(a0, a1, a2)
    return out[:3]


def place_kernel(blocks, weak, e0, e1, e2, schur, product, rhs, diag):
    xb = pl.program_id(0)
    row, col = lax.axis_index("row"), lax.axis_index("col")

    @pl.when(xb == 0)
    def _():
        schur[...] = jnp.zeros_like(schur)
        rhs[...] = jnp.zeros_like(rhs)

    def bundle(i, carry):
        y, z = i // 4, i % 4
        b = i * 8 + xb
        k = blocks[b, row]
        l0 = pl.multiple_of(blocks[b, 2 * col] * BW, BW)
        l1 = pl.multiple_of(blocks[b, 2 * col + 1] * BW + GB * BW, BW)
        r = pl.multiple_of(k * BW, BW)
        schur[pl.ds(r, 88), pl.ds(l0, BW)] += e0[0, z, y]
        schur[pl.ds(r + 88, 40), pl.ds(l0, BW)] += e1[y, 0, z, 0:40]
        schur[pl.ds(r, 48), pl.ds(l1, BW)] += e1[y, 0, z, 40:88]
        schur[pl.ds(r + 48, 80), pl.ds(l1, BW)] += e2[z, y, 0, 0:80]
        rhs[pl.ds(k, 1), :] += e2[z, y, 0, 80:81]
        return carry

    lax.fori_loop(0, 16, bundle, 0)

    @pl.when(xb == 7)
    def _():
        w = weak[...]
        w_hi = w.astype(bf16)
        w_lo = (w - w_hi.astype(f32)).astype(bf16)

        def multiply(i, carry):
            r = pl.ds(pl.multiple_of(i * BW, BW), BW)
            v = schur[r, :]
            hi = v.astype(bf16)
            lo = (v - hi.astype(f32)).astype(bf16)
            product[r, :] = nn(hi, w_hi) + nn(hi, w_lo) + nn(lo, w_hi)
            return carry

        lax.fori_loop(0, GB, multiply, 0)
        side = pl.multiple_of((row % 2) * GB * BW, GB * BW)

        def corner(k, carry):
            at = pl.multiple_of(k * BW, BW)
            diag[k] = schur[pl.ds(at, BW), pl.ds(pl.multiple_of(side + at, BW), BW)]
            return carry

        lax.fori_loop(0, GB, corner, 0)

        @pl.when(col == row // 2)
        def _():
            schur[:, pl.ds(side, GB * BW)] = jnp.zeros((GB * BW, GB * BW), f32)


def place(blocks, weak, e0, e1, e2):
    def whole(*shape):
        return pl.BlockSpec(shape, lambda i: (0,) * len(shape))

    return pl.pallas_call(
        place_kernel,
        grid=(8,),
        in_specs=[
            pl.BlockSpec(memory_space=pltpu.SMEM),
            whole(2 * GB * BW, 64),
            pl.BlockSpec((1, 4, 4, ROWS, BW), lambda i: (i, 0, 0, 0, 0)),
            pl.BlockSpec((4, 1, 4, ROWS, BW), lambda i: (0, i, 0, 0, 0)),
            pl.BlockSpec((4, 4, 1, ROWS, BW), lambda i: (0, 0, i, 0, 0)),
        ],
        out_specs=(
            whole(GB * BW, 2 * GB * BW),
            whole(GB * BW, 64),
            whole(GB, BW),
            whole(GB, BW, BW),
        ),
        out_shape=(
            jax.ShapeDtypeStruct((GB * BW, 2 * GB * BW), f32),
            jax.ShapeDtypeStruct((GB * BW, 64), f32),
            jax.ShapeDtypeStruct((GB, BW), f32),
            jax.ShapeDtypeStruct((GB, BW, BW), f32),
        ),
        compiler_params=pltpu.CompilerParams(
            dimension_semantics=("arbitrary",), vmem_limit_bytes=56 << 20
        ),
        name="place",
    )(blocks, weak, e0, e1, e2)


def finish_kernel(product, diag, layer, weak, got, tile, ssem, rsem, tsend, trecv):
    me = coords()
    row = lax.axis_index("row")
    mine = me["X"]
    owner = row // 2
    copies = []
    for o in WIDE:
        to = moved(me, "X", o, 1)
        cp = pltpu.make_async_remote_copy(
            src_ref=product.at[pl.ds(pl.multiple_of(to * BW, BW), BW), :],
            dst_ref=got.at[o],
            send_sem=ssem.at[o],
            recv_sem=rsem.at[o],
            device_id=device(me, "X", to),
            device_id_type=MESH,
        )
        cp.start()
        copies.append(cp)

    def hand(o):
        to = moved(me, "X", o, 1)
        return pltpu.make_async_remote_copy(
            src_ref=diag.at[to],
            dst_ref=tile,
            send_sem=tsend.at[o],
            recv_sem=trecv,
            device_id=device(me, "X", to),
            device_id_type=MESH,
        )

    @pl.when(mine == owner)
    def _():
        for o in WIDE:
            hand(o).start()

    layer[...] = jnp.zeros_like(layer)
    here = pl.ds(pl.multiple_of(mine * BW, BW), BW)
    weak[...] = product[here, :]

    @pl.when(mine != owner)
    def _():
        hand(1).wait_recv()
        layer[here, :] = tile[...]

    @pl.when(mine == owner)
    def _():
        layer[here, :] = diag[mine]

    for cp in copies:
        cp.wait_recv()
    total = weak[...]
    for o in WIDE:
        total = total + got[o]
    weak[...] = total
    for cp in copies:
        cp.wait_send()

    @pl.when(mine == owner)
    def _():
        for o in WIDE:
            hand(o).wait_send()


def finish(product, diag):
    vmem = pl.BlockSpec(memory_space=pltpu.VMEM)
    return pl.pallas_call(
        finish_kernel,
        out_shape=(
            jax.ShapeDtypeStruct((GB * BW, BW), f32),
            jax.ShapeDtypeStruct((BW, 64), f32),
        ),
        in_specs=[vmem] * 2,
        out_specs=(vmem,) * 2,
        scratch_shapes=[
            pltpu.VMEM((8, BW, 64), f32),
            pltpu.VMEM((BW, BW), f32),
            pltpu.SemaphoreType.DMA((8,)),
            pltpu.SemaphoreType.DMA((8,)),
            pltpu.SemaphoreType.DMA((8,)),
            pltpu.SemaphoreType.DMA,
        ],
        compiler_params=pltpu.CompilerParams(has_side_effects=True),
        name="finish",
    )(product, diag)


def body(glob_derivs, local_derivs, weights, residuals, track_ids, module_blocks, weak_modes):
    a = head(glob_derivs[0], local_derivs[0], weights[0], residuals[0], track_ids[0])
    e = exchange(*a)
    schur, product, rhs, diag = place(module_blocks, weak_modes, *e)
    layer, weak = finish(product, diag)
    return schur, layer, rhs.reshape(GB * BW), weak


def solution(mesh):
    placed = (
        P(("row", "col"), None, None, None),
        P(("row", "col"), None, None, None),
        P(("row", "col"), None, None),
        P(("row", "col"), None, None),
        P(("row", "col"), None, None),
        P(),
        P("col", None),
    )
    return jax.shard_map(
        body,
        mesh=mesh,
        in_specs=placed,
        out_specs=(P("row", "col"), P("row", "col"), P("row"), P(("row", "col"), None)),
        check_vma=False,
    )
```

```python
import functools

import jax
import jax.numpy as jnp
from jax import lax
from jax.experimental import pallas as pl
from jax.experimental.pallas import tpu as pltpu
from jax.sharding import PartitionSpec as P

BW = 128
GB = 8
LOC = 4
TRK = 256
LAYERS = 16
PER = 256
ROWS = (88, 88, 80)
SIZE = {"y": 4, "z": 4, "X": 8}
ORDERS = (("y", "z", "X"), ("z", "X", "y"), ("X", "y", "z"))
RING = (1, 3, 2)
WIDE = (2, 6, 3, 7, 4, 5, 1)
CHUNKS = (2, 6, 3, 7, 0, 4, 5, 1)
MESH = pl.DeviceIdType.MESH
f32 = jnp.float32
bf16 = jnp.bfloat16


def split3(v):
    hi = v.astype(bf16)
    rest = v - hi.astype(f32)
    mid = rest.astype(bf16)
    low = (rest - mid.astype(f32)).astype(bf16)
    return hi, mid, low


def nt(a, b):
    return lax.dot_general(a, b, (((1,), (1,)), ((), ())), preferred_element_type=f32)


def nn(a, b):
    return lax.dot_general(a, b, (((1,), (0,)), ((), ())), preferred_element_type=f32)


def local_terms(glob, local, weight, resid, tracks, h_all, x_all, d_all, v_all, sums, q_ref, k_ref):
    sums[...] = jnp.zeros_like(sums)

    def first(s, carry):
        g = glob[s]
        gt = jnp.transpose(g.astype(f32))
        gt_low = gt.astype(bf16)
        t = tracks[pl.ds(s, 1), :]
        w = weight[pl.ds(s, 1), :]
        r = resid[pl.ds(s, 1), :]
        hot = lax.broadcasted_iota(jnp.int32, (TRK, PER), 0) == t
        a = local[s]
        wa = w * a
        zero = jnp.zeros((), f32)
        row = pl.ds(pl.multiple_of(s * BW, BW), BW)
        for j in range(LOC):
            spread = jnp.where(hot, wa[j : j + 1, :], zero).astype(bf16)
            h_all[row, j * TRK : (j + 1) * TRK] = nt(gt_low, spread).astype(bf16)
        terms = []
        for i in range(LOC):
            terms.append(wa[i : i + 1, :] * a)
        terms.append(wa * r)
        terms.append(jnp.zeros((4, PER), f32))
        stacked = jnp.concatenate(terms, axis=0)
        hot_low = jnp.where(hot, jnp.ones((), f32), zero).astype(bf16)
        hi, mid, low = split3(stacked)
        sums[...] += nt(hi, hot_low) + nt(mid, hot_low) + nt(low, hot_low)
        d_all[row, :] = nn((gt * w).astype(bf16), g)
        wr = jnp.broadcast_to((w * r).astype(bf16), (16, PER))
        v_all[s // 4, s % 4] = nn(wr, g)[:8]
        return carry

    lax.fori_loop(0, LAYERS, first, 0)

    one = jnp.ones((1, TRK), f32)
    nil = jnp.zeros((1, TRK), f32)
    rows = [
        [sums[4 * i + j : 4 * i + j + 1, :] + (one if i == j else nil) for j in range(LOC)]
        for i in range(LOC)
    ]
    inv = [[one if i == j else nil for j in range(LOC)] for i in range(LOC)]
    for p in range(LOC):
        pivot = rows[p][p]
        scaled = [v / pivot for v in rows[p]]
        scaled_inv = [v / pivot for v in inv[p]]
        for o in range(LOC):
            if o != p:
                factor = rows[o][p]
                rows[o] = [u - factor * v for u, v in zip(rows[o], scaled)]
                inv[o] = [u - factor * v for u, v in zip(inv[o], scaled_inv)]
        rows[p] = scaled
        inv[p] = scaled_inv
    for i in range(LOC):
        for j in range(LOC):
            k_ref[4 * i + j : 4 * i + j + 1, :] = inv[i][j]
    for j in range(LOC):
        q_ref[:, j * TRK : (j + 1) * TRK] = jnp.broadcast_to(
            sums[16 + j : 17 + j, :].astype(bf16), (16, TRK)
        )

    def second(s, carry):
        row = pl.ds(pl.multiple_of(s * BW, BW), BW)
        h = [h_all[row, l * TRK : (l + 1) * TRK].astype(f32) for l in range(LOC)]
        for j in range(LOC):
            x = h[0] * k_ref[j : j + 1, :]
            for l in range(1, LOC):
                x = x + h[l] * k_ref[4 * l + j : 4 * l + j + 1, :]
            x_all[row, j * TRK : (j + 1) * TRK] = (-x).astype(bf16)
        v_all[s // 4, s % 4] = v_all[s // 4, s % 4] + nt(q_ref[...], x_all[row, :])[:8]
        return carry

    lax.fori_loop(0, LAYERS, second, 0)


def tiles_for(c, a0, a1, a2, h_all, x_all, d_all):
    right = h_all[pl.ds(pl.multiple_of(c * 2 * BW, 2 * BW), 2 * BW), :]

    def gram(y, carry):
        out = nt(x_all[pl.ds(pl.multiple_of(y * 4 * BW, 4 * BW), 4 * BW), :], right)
        for z in range(4):
            part = out[z * BW : (z + 1) * BW, :]
            a0[y, z, c] = part[0:88, :BW]
            a1[z, c, y, 0:40] = part[88:BW, :BW]
            a1[z, c, y, 40:88] = part[0:48, BW:]
            a2[c, y, z] = part[48:BW, BW:]
        return carry

    lax.fori_loop(0, 4, gram, 0)
    s = 2 * c
    y, z = s // 4, s % 4
    base = pl.multiple_of(s * BW, BW)
    a0[y, z, c] += d_all[pl.ds(base, 88), :]
    a1[z, c, y, 0:40] += d_all[pl.ds(base + 88, 40), :]
    base = pl.multiple_of(s * BW + BW, BW)
    a1[z + 1, c, y, 40:88] += d_all[pl.ds(base, 48), :]
    a2[c, y, z + 1] += d_all[pl.ds(base + 48, 80), :]


def coords():
    r, c = lax.axis_index("row"), lax.axis_index("col")
    return {"y": r // 4, "z": r % 4, "X": c}


def moved(me, dim, offset, sign):
    if dim == "X":
        x, k = me["X"] // 2, me["X"] % 2
        dx, dk = offset // 2, offset % 2
        return ((x + 4 + sign * dx) % 4) * 2 + (k + dk) % 2
    return (me[dim] + 4 + sign * offset) % 4


def device(me, dim, place):
    at = dict(me)
    at[dim] = place
    return (at["y"] * 4 + at["z"], at["X"])


def offsets(dim):
    return WIDE if dim == "X" else RING


def greet(me, dims):
    barrier = pltpu.get_barrier_semaphore()
    count = 0
    for dim in dims:
        for o in offsets(dim):
            pl.semaphore_signal(
                barrier,
                inc=1,
                device_id=device(me, dim, moved(me, dim, o, 1)),
                device_id_type=MESH,
            )
            count += 1
    return barrier, count


def exchange_kernel(glob, local, weight, resid, tracks, *refs):
    e, v_out, b, cc = refs[0:3], refs[3], refs[4:7], refs[7:10]
    a = refs[10:13]
    bounce2, bounce3 = refs[13:16], refs[16:19]
    h_all, x_all, d_all, v_all, v_mid, sums, q_ref, k_ref = refs[19:27]
    s1, r1, s2, r2, s3, r3, lsem, vs, vr = refs[27:36]
    me = coords()
    barrier, count = greet(me, ("y", "z", "X"))
    local_terms(
        glob, local, weight, resid, tracks, h_all, x_all, d_all, v_all, sums, q_ref, k_ref
    )
    pl.semaphore_wait(barrier, count)
    sends = []

    def send(src, dst, ssem, rsem, dim, place):
        cp = pltpu.make_async_remote_copy(
            src_ref=src,
            dst_ref=dst,
            send_sem=ssem,
            recv_sem=rsem,
            device_id=device(me, dim, place),
            device_id_type=MESH,
        )
        cp.start()
        sends.append(cp)
        return cp

    pending = []
    count = [0]

    def local_copy(src, mid, dst, done):
        into = pltpu.make_async_copy(src, mid, lsem.at[count[0]])
        out = pltpu.make_async_copy(mid, dst, lsem.at[count[0]])
        count[0] += 1
        into.start()
        pending.append((into, out))
        done.append(out)

    def flush():
        for into, out in pending:
            into.wait()
            out.start()
        pending.clear()

    fifth = {}

    def stage1(j):
        o = CHUNKS[j]
        c = moved(me, "X", o, 1)
        for oo in RING:
            to = moved(me, "y", oo, 1)
            send(a[0].at[to, :, c], b[0].at[me["y"], :, c], s1.at[0, oo, j], r1.at[0, oo, j], "y", to)
            to = moved(me, "z", oo, 1)
            send(a[1].at[to, c], b[1].at[me["z"], c], s1.at[1, oo, j], r1.at[1, oo, j], "z", to)
        if o:
            send(a[2].at[c], b[2].at[me["X"]], s1.at[2, o, 0], r1.at[2, o, 0], "X", c)

    for j, o in enumerate(CHUNKS):
        tiles_for(moved(me, "X", o, 1), *a, h_all, x_all, d_all)
        if j:
            stage1(j - 1)
    for oo in RING:
        to = moved(me, "y", oo, 1)
        fifth[oo] = send(v_all.at[to], v_mid.at[me["y"]], vs.at[0, oo], vr.at[0, oo], "y", to)
    v_mid[me["y"]] = v_all[me["y"]]
    stage1(7)

    def arrived1(g, o):
        src = moved(me, ORDERS[g][0], o, -1)
        if g == 2:
            pltpu.make_async_copy(b[2].at[src], b[2].at[src], r1.at[2, o, 0]).wait()
            return
        for j, oc in enumerate(CHUNKS):
            c = moved(me, "X", oc, 1)
            ref = b[0].at[src, :, c] if g == 0 else b[1].at[src, c]
            pltpu.make_async_copy(ref, ref, r1.at[g, o, j]).wait()

    second = {}
    back2 = {}
    for step in range(8):
        for g, order in enumerate(ORDERS):
            d1, d2, _ = order
            offs = (0,) + offsets(d1)
            if step >= len(offs):
                continue
            o1 = offs[step]
            src1 = moved(me, d1, o1, -1)
            if o1:
                arrived1(g, o1)
            for o2 in offsets(d2):
                to = moved(me, d2, o2, 1)
                src = b[g].at[src1, to] if o1 else a[g].at[me[d1], to]
                second[g, o1, o2] = send(
                    src, cc[g].at[me[d2], src1], s2.at[g, o1, o2], r2.at[g, o1, o2], d2, to
                )
            flush()
            done = back2.setdefault(g, [])
            if o1:
                local_copy(b[g].at[src1, me[d2]], bounce2[g].at[o1], cc[g].at[me[d2], src1], done)
            else:
                out = pltpu.make_async_copy(
                    a[g].at[me[d1], me[d2]], cc[g].at[me[d2], src1], lsem.at[count[0]]
                )
                count[0] += 1
                out.start()
                done.append(out)
    for oo in RING:
        fifth[oo].wait_recv()
    v_last = {}
    for oo in RING:
        to = moved(me, "z", oo, 1)
        v_last[oo] = send(v_mid.at[:, to], v_out.at[me["z"]], vs.at[1, oo], vr.at[1, oo], "z", to)
    v_out[me["z"]] = v_mid[:, me["z"]]
    flush()
    third = []
    last = []
    for step in range(8):
        for g, order in enumerate(ORDERS):
            d1, d2, d3 = order
            offs = (0,) + offsets(d2)
            if step >= len(offs):
                continue
            o2 = offs[step]
            src2 = moved(me, d2, o2, -1)
            if o2:
                for o1 in (0,) + offsets(d1):
                    second[g, o1, o2].wait_recv()
            else:
                for out in back2[g]:
                    out.wait()
            for o3 in offsets(d3):
                to = moved(me, d3, o3, 1)
                third.append(
                    send(
                        cc[g].at[src2, :, to],
                        e[g].at[me[d3], src2],
                        s3.at[g, o2, o3],
                        r3.at[g, o2, o3],
                        d3,
                        to,
                    )
                )
            flush()
            local_copy(cc[g].at[src2, :, me[d3]], bounce3[g].at[o2], e[g].at[me[d3], src2], last)
    flush()
    for oo in RING:
        v_last[oo].wait_recv()
    for cp in last:
        cp.wait()
    for cp in third:
        cp.wait_recv()
    for cp in sends:
        cp.wait_send()


def exchange(glob, local, weight, resid, tracks):
    sizes = [tuple(SIZE[d] for d in order) for order in ORDERS]
    items = [(rows, BW) for rows in ROWS]
    both = list(zip(sizes, items))
    shapes = (
        [jax.ShapeDtypeStruct((n3, n2, n1) + it, f32) for (n1, n2, n3), it in both]
        + [jax.ShapeDtypeStruct((4, 4, 8, BW), f32)]
        + [jax.ShapeDtypeStruct((n1, n2, n3) + it, f32) for (n1, n2, n3), it in both]
        + [jax.ShapeDtypeStruct((n2, n1, n3) + it, f32) for (n1, n2, n3), it in both]
    )
    any_ = pl.BlockSpec(memory_space=pl.ANY)
    vmem = pl.BlockSpec(memory_space=pltpu.VMEM)
    out = pl.pallas_call(
        exchange_kernel,
        out_shape=tuple(shapes),
        in_specs=[vmem] * 5,
        out_specs=(any_,) * 3 + (vmem,) + (any_,) * 6,
        scratch_shapes=[pltpu.VMEM(n + it, f32) for n, it in both]
        + [pltpu.VMEM((n1, n3) + it, f32) for (n1, n2, n3), it in both]
        + [pltpu.VMEM((n2, n1) + it, f32) for (n1, n2, n3), it in both]
        + [
            pltpu.VMEM((LAYERS * BW, LOC * TRK), bf16),
            pltpu.VMEM((LAYERS * BW, LOC * TRK), bf16),
            pltpu.VMEM((LAYERS * BW, BW), f32),
            pltpu.VMEM((4, 4, 8, BW), f32),
            pltpu.VMEM((4, 4, 8, BW), f32),
            pltpu.VMEM((24, TRK), f32),
            pltpu.VMEM((16, LOC * TRK), bf16),
            pltpu.VMEM((16, TRK), f32),
            pltpu.SemaphoreType.DMA((3, 8, 8)),
            pltpu.SemaphoreType.DMA((3, 8, 8)),
            pltpu.SemaphoreType.DMA((3, 8, 8)),
            pltpu.SemaphoreType.DMA((3, 8, 8)),
            pltpu.SemaphoreType.DMA((3, 8, 8)),
            pltpu.SemaphoreType.DMA((3, 8, 8)),
            pltpu.SemaphoreType.DMA((32,)),
            pltpu.SemaphoreType.DMA((2, 4)),
            pltpu.SemaphoreType.DMA((2, 4)),
        ],
        compiler_params=pltpu.CompilerParams(
            collective_id=0, has_side_effects=True, vmem_limit_bytes=60 << 20
        ),
        name="exchange",
    )(glob, local, weight, resid, tracks)
    return out[:4]


def place_kernel(blocks, weak, e0, e1, e2, vec, schur, product, rhs, diag, acc, w_ref, p_ref, sem):
    xb = pl.program_id(0)
    row, col = lax.axis_index("row"), lax.axis_index("col")

    @pl.when(xb == 0)
    def _():
        acc[...] = jnp.zeros_like(acc)
        rhs[...] = jnp.zeros_like(rhs)

        def term(i, carry):
            k = blocks[row, i * 8 + col]
            rhs[pl.ds(k, 1), :] += vec[i % 4, i // 4, 0:1]
            return carry

        lax.fori_loop(0, 16, term, 0)

    def bundle(i, carry):
        y, z = i // 4, i % 4
        b = i * 8 + xb
        l0 = pl.multiple_of(blocks[2 * col, b] * BW, BW)
        l1 = pl.multiple_of(blocks[2 * col + 1, b] * BW + GB * BW, BW)
        r = pl.multiple_of(blocks[row, b] * BW, BW)
        acc[pl.ds(r, 88), pl.ds(l0, BW)] += e0[0, z, y]
        acc[pl.ds(r + 88, 40), pl.ds(l0, BW)] += e1[y, 0, z, 0:40]
        acc[pl.ds(r, 48), pl.ds(l1, BW)] += e1[y, 0, z, 40:88]
        acc[pl.ds(r + 48, 80), pl.ds(l1, BW)] += e2[z, y, 0]
        return carry

    lax.fori_loop(0, 16, bundle, 0)

    @pl.when(xb == 7)
    def _():
        w = weak[...]
        w_hi = w.astype(bf16)
        w_ref[0:64, :] = w_hi
        w_ref[64:128, :] = (w - w_hi.astype(f32)).astype(bf16)
        p_ref[...] = jnp.zeros_like(p_ref)

        def copy_out(ch):
            cols = pl.ds(pl.multiple_of(ch * 256, 256), 256)
            return pltpu.make_async_copy(acc.at[:, cols], schur.at[:, cols], sem.at[ch])

        def chunk(ch, carry):
            cols = pl.ds(pl.multiple_of(ch * 256, 256), 256)
            wc = w_ref[:, cols]

            def multiply(i, carry):
                r = pl.ds(pl.multiple_of(i * 256, 256), 256)
                v = acc[r, cols]
                hi = v.astype(bf16)
                lo = (v - hi.astype(f32)).astype(bf16)
                p_ref[r, :] += nt(hi, wc) + nt(lo, wc)
                return carry

            lax.fori_loop(0, 4, multiply, 0)

            @pl.when(ch // 4 == row % 2)
            def _():
                for m in range(2):
                    k = 2 * (ch % 4) + m
                    diag[k] = acc[
                        pl.ds(pl.multiple_of(k * BW, BW), BW),
                        pl.ds(pl.multiple_of(ch * 256 + m * BW, BW), BW),
                    ]

                @pl.when(col == row // 2)
                def _():
                    acc[:, cols] = jnp.zeros((GB * BW, 256), f32)

            copy_out(ch).start()
            return carry

        lax.fori_loop(0, 8, chunk, 0)
        for k in range(GB):
            pt = jnp.transpose(p_ref[k * BW : (k + 1) * BW, :])
            product[k] = pt[0:64] + pt[64:128]
        for ch in range(8):
            copy_out(ch).wait()


def place(blocks, weak, e0, e1, e2, vec):
    def whole(*shape):
        return pl.BlockSpec(shape, lambda i: (0,) * len(shape))

    r0, r1, r2 = ROWS
    return pl.pallas_call(
        place_kernel,
        grid=(8,),
        in_specs=[
            pl.BlockSpec(memory_space=pltpu.SMEM),
            whole(64, 2 * GB * BW),
            pl.BlockSpec((1, 4, 4, r0, BW), lambda i: (i, 0, 0, 0, 0)),
            pl.BlockSpec((4, 1, 4, r1, BW), lambda i: (0, i, 0, 0, 0)),
            pl.BlockSpec((4, 4, 1, r2, BW), lambda i: (0, 0, i, 0, 0)),
            whole(4, 4, 8, BW),
        ],
        out_specs=(
            pl.BlockSpec(memory_space=pl.ANY),
            whole(GB, 64, BW),
            whole(GB, BW),
            whole(GB, BW, BW),
        ),
        out_shape=(
            jax.ShapeDtypeStruct((GB * BW, 2 * GB * BW), f32),
            jax.ShapeDtypeStruct((GB, 64, BW), f32),
            jax.ShapeDtypeStruct((GB, BW), f32),
            jax.ShapeDtypeStruct((GB, BW, BW), f32),
        ),
        scratch_shapes=[
            pltpu.VMEM((GB * BW, 2 * GB * BW), f32),
            pltpu.VMEM((BW, 2 * GB * BW), bf16),
            pltpu.VMEM((GB * BW, BW), f32),
            pltpu.SemaphoreType.DMA((8,)),
        ],
        compiler_params=pltpu.CompilerParams(
            dimension_semantics=("arbitrary",), vmem_limit_bytes=56 << 20
        ),
        name="place",
    )(blocks, weak, e0, e1, e2, vec)


def finish_kernel(product, diag, part, weak, tile, rhs, got, got_r, ssem, rsem, tsend, trecv):
    me = coords()
    row = lax.axis_index("row")
    mine = me["X"]
    owner = row // 2
    barrier, count = greet(me, ("X",))
    pl.semaphore_wait(barrier, count)
    copies = []
    for o in WIDE:
        to = moved(me, "X", o, 1)
        for i, (src, dst) in enumerate(((product.at[to], got.at[o]), (part, got_r.at[o]))):
            cp = pltpu.make_async_remote_copy(
                src_ref=src,
                dst_ref=dst,
                send_sem=ssem.at[i, o],
                recv_sem=rsem.at[i, o],
                device_id=device(me, "X", to),
                device_id_type=MESH,
            )
            cp.start()
            copies.append(cp)

    def hand(o):
        to = moved(me, "X", o, 1)
        return pltpu.make_async_remote_copy(
            src_ref=diag.at[to],
            dst_ref=tile,
            send_sem=tsend.at[o],
            recv_sem=trecv,
            device_id=device(me, "X", to),
            device_id_type=MESH,
        )

    @pl.when(mine == owner)
    def _():
        for o in WIDE:
            hand(o).start()
        tile[...] = diag[mine]

    for cp in copies:
        cp.wait_recv()
    total = product[mine]
    total_r = part[...]
    for o in WIDE:
        total = total + got[o]
        total_r = total_r + got_r[o]
    weak[...] = total
    rhs[...] = total_r
    for cp in copies:
        cp.wait_send()

    @pl.when(mine != owner)
    def _():
        hand(1).wait_recv()

    @pl.when(mine == owner)
    def _():
        for o in WIDE:
            hand(o).wait_send()


def finish(product, diag, part):
    vmem = pl.BlockSpec(memory_space=pltpu.VMEM)
    return pl.pallas_call(
        finish_kernel,
        out_shape=(
            jax.ShapeDtypeStruct((64, BW), f32),
            jax.ShapeDtypeStruct((BW, BW), f32),
            jax.ShapeDtypeStruct((GB, BW), f32),
        ),
        in_specs=[vmem] * 3,
        out_specs=(vmem,) * 3,
        scratch_shapes=[
            pltpu.VMEM((8, 64, BW), f32),
            pltpu.VMEM((8, GB, BW), f32),
            pltpu.SemaphoreType.DMA((2, 8)),
            pltpu.SemaphoreType.DMA((2, 8)),
            pltpu.SemaphoreType.DMA((8,)),
            pltpu.SemaphoreType.DMA,
        ],
        compiler_params=pltpu.CompilerParams(collective_id=1, has_side_effects=True),
        name="finish",
    )(product, diag, part)


def body(glob_derivs, local_derivs, weights, residuals, track_ids, module_blocks, weak_modes):
    e = exchange(glob_derivs[0], local_derivs[0], weights[0], residuals[0], track_ids[0])
    schur, product, part, diag = place(module_blocks.T, weak_modes.T, *e)
    weak, tile, rhs = finish(product, diag, part)
    here = jnp.arange(GB)[:, None, None] == lax.axis_index("col")
    layer = jnp.where(here, tile[None], jnp.zeros((), f32)).reshape(GB * BW, BW)
    return schur, layer, rhs.reshape(GB * BW), weak.T


def solution(mesh):
    placed = (
        P(("row", "col"), None, None, None),
        P(("row", "col"), None, None, None),
        P(("row", "col"), None, None),
        P(("row", "col"), None, None),
        P(("row", "col"), None, None),
        P(),
        P("col", None),
    )
    return jax.shard_map(
        body,
        mesh=mesh,
        in_specs=placed,
        out_specs=(P("row", "col"), P("row", "col"), P("row"), P(("row", "col"), None)),
        check_vma=False,
    )
```

```python
import functools

import jax
import jax.numpy as jnp
from jax import lax
from jax.experimental import pallas as pl
from jax.experimental.pallas import tpu as pltpu
from jax.sharding import PartitionSpec as P

BW = 128
GB = 8
LOC = 4
TRK = 256
LAYERS = 16
PER = 256
ROWS = (88, 88, 80)
SIZE = {"y": 4, "z": 4, "X": 8}
ORDERS = (("y", "z", "X"), ("z", "X", "y"), ("X", "y", "z"))
RING = (1, 3, 2)
WIDE = (2, 6, 3, 7, 4, 5, 1)
CHUNKS = (2, 6, 3, 7, 0, 4, 5, 1)
MESH = pl.DeviceIdType.MESH
f32 = jnp.float32
bf16 = jnp.bfloat16


def split3(v):
    hi = v.astype(bf16)
    rest = v - hi.astype(f32)
    mid = rest.astype(bf16)
    low = (rest - mid.astype(f32)).astype(bf16)
    return hi, mid, low


def nt(a, b):
    return lax.dot_general(a, b, (((1,), (1,)), ((), ())), preferred_element_type=f32)


def nn(a, b):
    return lax.dot_general(a, b, (((1,), (0,)), ((), ())), preferred_element_type=f32)


def local_terms(glob, local, weight, resid, tracks, h_all, x_all, d_all, v_all, sums, q_ref, k_ref):
    sums[...] = jnp.zeros_like(sums)

    def first(s, carry):
        g = glob[s]
        gt = jnp.transpose(g.astype(f32))
        gt_low = gt.astype(bf16)
        t = tracks[pl.ds(s, 1), :]
        w = weight[pl.ds(s, 1), :]
        r = resid[pl.ds(s, 1), :]
        hot = lax.broadcasted_iota(jnp.int32, (TRK, PER), 0) == t
        a = local[s]
        wa = w * a
        zero = jnp.zeros((), f32)
        row = pl.ds(pl.multiple_of(s * BW, BW), BW)
        for j in range(LOC):
            spread = jnp.where(hot, wa[j : j + 1, :], zero).astype(bf16)
            h_all[row, j * TRK : (j + 1) * TRK] = nt(gt_low, spread).astype(bf16)
        terms = []
        for i in range(LOC):
            terms.append(wa[i : i + 1, :] * a)
        terms.append(wa * r)
        terms.append(jnp.zeros((4, PER), f32))
        stacked = jnp.concatenate(terms, axis=0)
        hot_low = jnp.where(hot, jnp.ones((), f32), zero).astype(bf16)
        hi, mid, low = split3(stacked)
        sums[...] += nt(hi, hot_low) + nt(mid, hot_low) + nt(low, hot_low)
        d_all[row, :] = nn((gt * w).astype(bf16), g)
        wr = jnp.broadcast_to((w * r).astype(bf16), (16, PER))
        v_all[s // 4, s % 4] = nn(wr, g)[:8]
        return carry

    lax.fori_loop(0, LAYERS, first, 0)

    one = jnp.ones((1, TRK), f32)
    nil = jnp.zeros((1, TRK), f32)
    rows = [
        [sums[4 * i + j : 4 * i + j + 1, :] + (one if i == j else nil) for j in range(LOC)]
        for i in range(LOC)
    ]
    inv = [[one if i == j else nil for j in range(LOC)] for i in range(LOC)]
    for p in range(LOC):
        pivot = rows[p][p]
        scaled = [v / pivot for v in rows[p]]
        scaled_inv = [v / pivot for v in inv[p]]
        for o in range(LOC):
            if o != p:
                factor = rows[o][p]
                rows[o] = [u - factor * v for u, v in zip(rows[o], scaled)]
                inv[o] = [u - factor * v for u, v in zip(inv[o], scaled_inv)]
        rows[p] = scaled
        inv[p] = scaled_inv
    for i in range(LOC):
        for j in range(LOC):
            k_ref[4 * i + j : 4 * i + j + 1, :] = inv[i][j]
    for j in range(LOC):
        q_ref[:, j * TRK : (j + 1) * TRK] = jnp.broadcast_to(
            sums[16 + j : 17 + j, :].astype(bf16), (16, TRK)
        )

    def second(s, carry):
        row = pl.ds(pl.multiple_of(s * BW, BW), BW)
        h = [h_all[row, l * TRK : (l + 1) * TRK].astype(f32) for l in range(LOC)]
        for j in range(LOC):
            x = h[0] * k_ref[j : j + 1, :]
            for l in range(1, LOC):
                x = x + h[l] * k_ref[4 * l + j : 4 * l + j + 1, :]
            x_all[row, j * TRK : (j + 1) * TRK] = (-x).astype(bf16)
        v_all[s // 4, s % 4] = v_all[s // 4, s % 4] + nt(q_ref[...], x_all[row, :])[:8]
        return carry

    lax.fori_loop(0, LAYERS, second, 0)


def tiles_for(c, a0, a1, a2, h_all, x_all, d_all):
    right = h_all[pl.ds(pl.multiple_of(c * 2 * BW, 2 * BW), 2 * BW), :]

    def gram(y, carry):
        out = nt(x_all[pl.ds(pl.multiple_of(y * 4 * BW, 4 * BW), 4 * BW), :], right)
        for z in range(4):
            part = out[z * BW : (z + 1) * BW, :]
            a0[y, z, c] = part[0:88, :BW]
            a1[z, c, y, 0:40] = part[88:BW, :BW]
            a1[z, c, y, 40:88] = part[0:48, BW:]
            a2[c, y, z] = part[48:BW, BW:]
        return carry

    lax.fori_loop(0, 4, gram, 0)
    s = 2 * c
    y, z = s // 4, s % 4
    base = pl.multiple_of(s * BW, BW)
    a0[y, z, c] += d_all[pl.ds(base, 88), :]
    a1[z, c, y, 0:40] += d_all[pl.ds(base + 88, 40), :]
    base = pl.multiple_of(s * BW + BW, BW)
    a1[z + 1, c, y, 40:88] += d_all[pl.ds(base, 48), :]
    a2[c, y, z + 1] += d_all[pl.ds(base + 48, 80), :]


def coords():
    r, c = lax.axis_index("row"), lax.axis_index("col")
    return {"y": r // 4, "z": r % 4, "X": c}


def moved(me, dim, offset, sign):
    if dim == "X":
        x, k = me["X"] // 2, me["X"] % 2
        dx, dk = offset // 2, offset % 2
        return ((x + 4 + sign * dx) % 4) * 2 + (k + dk) % 2
    return (me[dim] + 4 + sign * offset) % 4


def device(me, dim, place):
    at = dict(me)
    at[dim] = place
    return (at["y"] * 4 + at["z"], at["X"])


def offsets(dim):
    return WIDE if dim == "X" else RING


def greet(me, dims):
    barrier = pltpu.get_barrier_semaphore()
    count = 0
    for dim in dims:
        for o in offsets(dim):
            pl.semaphore_signal(
                barrier,
                inc=1,
                device_id=device(me, dim, moved(me, dim, o, 1)),
                device_id_type=MESH,
            )
            count += 1
    return barrier, count


def exchange_kernel(glob, local, weight, resid, tracks, *refs):
    e, v_out, b, cc = refs[0:3], refs[3], refs[4:7], refs[7:10]
    a = refs[10:13]
    bounce2, bounce3 = refs[13:16], refs[16:19]
    h_all, x_all, d_all, v_all, v_mid, sums, q_ref, k_ref = refs[19:27]
    ssem, r1, r2, r3, into_sem, out_sem, v_sem = refs[27:34]
    me = coords()
    barrier, count = greet(me, ("y", "z", "X"))
    local_terms(
        glob, local, weight, resid, tracks, h_all, x_all, d_all, v_all, sums, q_ref, k_ref
    )
    pl.semaphore_wait(barrier, count)

    def send(src, dst, ssem, rsem, dim, place):
        cp = pltpu.make_async_remote_copy(
            src_ref=src,
            dst_ref=dst,
            send_sem=ssem,
            recv_sem=rsem,
            device_id=device(me, dim, place),
            device_id_type=MESH,
        )
        cp.start()

    def wait_for(ref, sem):
        pltpu.make_async_copy(ref, ref, sem).wait()

    pending = []

    def local_copy(src, mid, dst, sem):
        into = pltpu.make_async_copy(src, mid, into_sem)
        into.start()
        pending.append((into, pltpu.make_async_copy(mid, dst, sem)))

    def flush():
        for into, out in pending:
            into.wait()
            out.start()
        pending.clear()

    def stage1(j):
        o = CHUNKS[j]
        c = moved(me, "X", o, 1)
        for oo in RING:
            to = moved(me, "y", oo, 1)
            send(a[0].at[to, :, c], b[0].at[me["y"], :, c], ssem.at[0, 0], r1.at[0, oo], "y", to)
            to = moved(me, "z", oo, 1)
            send(a[1].at[to, c], b[1].at[me["z"], c], ssem.at[0, 1], r1.at[1, oo], "z", to)
        if o:
            send(a[2].at[c], b[2].at[me["X"]], ssem.at[0, 2], r1.at[2, o], "X", c)

    for j, o in enumerate(CHUNKS):
        tiles_for(moved(me, "X", o, 1), *a, h_all, x_all, d_all)
        if j:
            stage1(j - 1)
    for oo in RING:
        to = moved(me, "y", oo, 1)
        send(v_all.at[to], v_mid.at[me["y"]], v_sem.at[0], v_sem.at[1], "y", to)
    v_mid[me["y"]] = v_all[me["y"]]
    stage1(7)

    for step in range(8):
        for g, order in enumerate(ORDERS):
            d1, d2, _ = order
            offs = (0,) + offsets(d1)
            if step >= len(offs):
                continue
            o1 = offs[step]
            src1 = moved(me, d1, o1, -1)
            if o1:
                wait_for(b[g].at[src1], r1.at[g, o1])
            for o2 in offsets(d2):
                to = moved(me, d2, o2, 1)
                src = b[g].at[src1, to] if o1 else a[g].at[me[d1], to]
                send(src, cc[g].at[me[d2], src1], ssem.at[1, g], r2.at[g, o2], d2, to)
            flush()
            back = cc[g].at[me[d2], src1]
            if o1:
                local_copy(b[g].at[src1, me[d2]], bounce2[g].at[o1], back, out_sem.at[0, g])
            else:
                pltpu.make_async_copy(a[g].at[me[d1], me[d2]], back, out_sem.at[0, g]).start()
    wait_for(v_mid.at[0:3], v_sem.at[1])
    for oo in RING:
        to = moved(me, "z", oo, 1)
        send(v_mid.at[:, to], v_out.at[me["z"]], v_sem.at[2], v_sem.at[3], "z", to)
    v_out[me["z"]] = v_mid[:, me["z"]]
    flush()
    for step in range(8):
        for g, order in enumerate(ORDERS):
            d1, d2, d3 = order
            offs = (0,) + offsets(d2)
            if step >= len(offs):
                continue
            o2 = offs[step]
            src2 = moved(me, d2, o2, -1)
            wait_for(cc[g].at[src2], r2.at[g, o2] if o2 else out_sem.at[0, g])
            for o3 in offsets(d3):
                to = moved(me, d3, o3, 1)
                send(
                    cc[g].at[src2, :, to],
                    e[g].at[me[d3], src2],
                    ssem.at[2, g],
                    r3.at[g],
                    d3,
                    to,
                )
            flush()
            local_copy(
                cc[g].at[src2, :, me[d3]],
                bounce3[g].at[o2],
                e[g].at[me[d3], src2],
                out_sem.at[1, g],
            )
    flush()
    wait_for(v_mid.at[0:3], v_sem.at[3])
    for g, order in enumerate(ORDERS):
        n1, n2, n3 = (SIZE[d] for d in order)
        wait_for(e[g].at[me[order[2]]], out_sem.at[1, g])
        wait_for(e[g].at[0 : n3 - 1], r3.at[g])
        wait_for(b[g].at[0 : n1 - 1], ssem.at[0, g])
        wait_for(cc[g].at[0 : n2 - 1], ssem.at[1, g])
        wait_for(e[g].at[0 : n3 - 1], ssem.at[2, g])
    wait_for(v_mid.at[0:3], v_sem.at[0])
    wait_for(v_mid.at[0:3], v_sem.at[2])


def exchange(glob, local, weight, resid, tracks):
    sizes = [tuple(SIZE[d] for d in order) for order in ORDERS]
    items = [(rows, BW) for rows in ROWS]
    both = list(zip(sizes, items))
    shapes = (
        [jax.ShapeDtypeStruct((n3, n2, n1) + it, f32) for (n1, n2, n3), it in both]
        + [jax.ShapeDtypeStruct((4, 4, 8, BW), f32)]
        + [jax.ShapeDtypeStruct((n1, n2, n3) + it, f32) for (n1, n2, n3), it in both]
        + [jax.ShapeDtypeStruct((n2, n1, n3) + it, f32) for (n1, n2, n3), it in both]
    )
    any_ = pl.BlockSpec(memory_space=pl.ANY)
    vmem = pl.BlockSpec(memory_space=pltpu.VMEM)
    out = pl.pallas_call(
        exchange_kernel,
        out_shape=tuple(shapes),
        in_specs=[vmem] * 5,
        out_specs=(any_,) * 3 + (vmem,) + (any_,) * 6,
        scratch_shapes=[pltpu.VMEM(n + it, f32) for n, it in both]
        + [pltpu.VMEM((n1, n3) + it, f32) for (n1, n2, n3), it in both]
        + [pltpu.VMEM((n2, n1) + it, f32) for (n1, n2, n3), it in both]
        + [
            pltpu.VMEM((LAYERS * BW, LOC * TRK), bf16),
            pltpu.VMEM((LAYERS * BW, LOC * TRK), bf16),
            pltpu.VMEM((LAYERS * BW, BW), f32),
            pltpu.VMEM((4, 4, 8, BW), f32),
            pltpu.VMEM((4, 4, 8, BW), f32),
            pltpu.VMEM((24, TRK), f32),
            pltpu.VMEM((16, LOC * TRK), bf16),
            pltpu.VMEM((16, TRK), f32),
            pltpu.SemaphoreType.DMA((3, 3)),
            pltpu.SemaphoreType.DMA((3, 8)),
            pltpu.SemaphoreType.DMA((3, 8)),
            pltpu.SemaphoreType.DMA((3,)),
            pltpu.SemaphoreType.DMA,
            pltpu.SemaphoreType.DMA((2, 3)),
            pltpu.SemaphoreType.DMA((4,)),
        ],
        compiler_params=pltpu.CompilerParams(
            collective_id=0, has_side_effects=True, vmem_limit_bytes=60 << 20
        ),
        name="exchange",
    )(glob, local, weight, resid, tracks)
    return out[:4]


def place_kernel(blocks, weak, e0, e1, e2, vec, schur, product, rhs, diag, acc, w_ref, p_ref, sem):
    xb = pl.program_id(0)
    row, col = lax.axis_index("row"), lax.axis_index("col")

    @pl.when(xb == 0)
    def _():
        acc[...] = jnp.zeros_like(acc)
        rhs[...] = jnp.zeros_like(rhs)

        def term(i, carry):
            k = blocks[row, i * 8 + col]
            rhs[pl.ds(k, 1), :] += vec[i % 4, i // 4, 0:1]
            return carry

        lax.fori_loop(0, 16, term, 0)

    def bundle(i, carry):
        y, z = i // 4, i % 4
        b = i * 8 + xb
        l0 = pl.multiple_of(blocks[2 * col, b] * BW, BW)
        l1 = pl.multiple_of(blocks[2 * col + 1, b] * BW + GB * BW, BW)
        r = pl.multiple_of(blocks[row, b] * BW, BW)
        acc[pl.ds(r, 88), pl.ds(l0, BW)] += e0[0, z, y]
        acc[pl.ds(r + 88, 40), pl.ds(l0, BW)] += e1[y, 0, z, 0:40]
        acc[pl.ds(r, 48), pl.ds(l1, BW)] += e1[y, 0, z, 40:88]
        acc[pl.ds(r + 48, 80), pl.ds(l1, BW)] += e2[z, y, 0]
        return carry

    lax.fori_loop(0, 16, bundle, 0)

    @pl.when(xb == 7)
    def _():
        w = weak[...]
        w_hi = w.astype(bf16)
        w_ref[0:64, :] = w_hi
        w_ref[64:128, :] = (w - w_hi.astype(f32)).astype(bf16)
        p_ref[...] = jnp.zeros_like(p_ref)

        def copy_out(ch):
            cols = pl.ds(pl.multiple_of(ch * 256, 256), 256)
            return pltpu.make_async_copy(acc.at[:, cols], schur.at[:, cols], sem.at[ch])

        def chunk(ch, carry):
            cols = pl.ds(pl.multiple_of(ch * 256, 256), 256)
            wc = w_ref[:, cols]

            def multiply(i, carry):
                r = pl.ds(pl.multiple_of(i * 256, 256), 256)
                v = acc[r, cols]
                hi = v.astype(bf16)
                lo = (v - hi.astype(f32)).astype(bf16)
                p_ref[r, :] += nt(hi, wc) + nt(lo, wc)
                return carry

            lax.fori_loop(0, 4, multiply, 0)

            @pl.when(ch // 4 == row % 2)
            def _():
                for m in range(2):
                    k = 2 * (ch % 4) + m
                    diag[k] = acc[
                        pl.ds(pl.multiple_of(k * BW, BW), BW),
                        pl.ds(pl.multiple_of(ch * 256 + m * BW, BW), BW),
                    ]

                @pl.when(col == row // 2)
                def _():
                    acc[:, cols] = jnp.zeros((GB * BW, 256), f32)

            copy_out(ch).start()
            return carry

        lax.fori_loop(0, 8, chunk, 0)
        for k in range(GB):
            pt = jnp.transpose(p_ref[k * BW : (k + 1) * BW, :])
            product[k] = pt[0:64] + pt[64:128]
        for ch in range(8):
            copy_out(ch).wait()


def place(blocks, weak, e0, e1, e2, vec):
    def whole(*shape):
        return pl.BlockSpec(shape, lambda i: (0,) * len(shape))

    r0, r1, r2 = ROWS
    return pl.pallas_call(
        place_kernel,
        grid=(8,),
        in_specs=[
            pl.BlockSpec(memory_space=pltpu.SMEM),
            whole(64, 2 * GB * BW),
            pl.BlockSpec((1, 4, 4, r0, BW), lambda i: (i, 0, 0, 0, 0)),
            pl.BlockSpec((4, 1, 4, r1, BW), lambda i: (0, i, 0, 0, 0)),
            pl.BlockSpec((4, 4, 1, r2, BW), lambda i: (0, 0, i, 0, 0)),
            whole(4, 4, 8, BW),
        ],
        out_specs=(
            pl.BlockSpec(memory_space=pl.ANY),
            whole(GB, 64, BW),
            whole(GB, BW),
            whole(GB, BW, BW),
        ),
        out_shape=(
            jax.ShapeDtypeStruct((GB * BW, 2 * GB * BW), f32),
            jax.ShapeDtypeStruct((GB, 64, BW), f32),
            jax.ShapeDtypeStruct((GB, BW), f32),
            jax.ShapeDtypeStruct((GB, BW, BW), f32),
        ),
        scratch_shapes=[
            pltpu.VMEM((GB * BW, 2 * GB * BW), f32),
            pltpu.VMEM((BW, 2 * GB * BW), bf16),
            pltpu.VMEM((GB * BW, BW), f32),
            pltpu.SemaphoreType.DMA((8,)),
        ],
        compiler_params=pltpu.CompilerParams(
            dimension_semantics=("arbitrary",), vmem_limit_bytes=56 << 20
        ),
        name="place",
    )(blocks, weak, e0, e1, e2, vec)


def finish_kernel(product, diag, part, weak, tile, rhs, got, got_r, ssem, rsem):
    me = coords()
    row = lax.axis_index("row")
    mine = me["X"]
    owner = row // 2
    barrier, count = greet(me, ("X",))
    pl.semaphore_wait(barrier, count)

    def copy(src, dst, i, to):
        return pltpu.make_async_remote_copy(
            src_ref=src,
            dst_ref=dst,
            send_sem=ssem.at[i],
            recv_sem=rsem.at[i],
            device_id=device(me, "X", to),
            device_id_type=MESH,
        )

    def wait_for(ref, sem):
        pltpu.make_async_copy(ref, ref, sem).wait()

    for o in WIDE:
        to = moved(me, "X", o, 1)
        copy(product.at[to], got.at[o - 1], 0, to).start()
        copy(part, got_r.at[o - 1], 1, to).start()

    @pl.when(mine == owner)
    def _():
        for o in WIDE:
            to = moved(me, "X", o, 1)
            copy(diag.at[to], tile, 2, to).start()
        tile[...] = diag[mine]

    wait_for(got, rsem.at[0])
    wait_for(got_r, rsem.at[1])
    total = product[mine]
    total_r = part[...]
    for o in range(7):
        total = total + got[o]
        total_r = total_r + got_r[o]
    weak[...] = total
    rhs[...] = total_r
    wait_for(got, ssem.at[0])
    wait_for(got_r, ssem.at[1])

    @pl.when(mine != owner)
    def _():
        wait_for(tile, rsem.at[2])

    @pl.when(mine == owner)
    def _():
        wait_for(diag.at[0:7], ssem.at[2])


def finish(product, diag, part):
    vmem = pl.BlockSpec(memory_space=pltpu.VMEM)
    return pl.pallas_call(
        finish_kernel,
        out_shape=(
            jax.ShapeDtypeStruct((64, BW), f32),
            jax.ShapeDtypeStruct((BW, BW), f32),
            jax.ShapeDtypeStruct((GB, BW), f32),
        ),
        in_specs=[vmem] * 3,
        out_specs=(vmem,) * 3,
        scratch_shapes=[
            pltpu.VMEM((7, 64, BW), f32),
            pltpu.VMEM((7, GB, BW), f32),
            pltpu.SemaphoreType.DMA((3,)),
            pltpu.SemaphoreType.DMA((3,)),
        ],
        compiler_params=pltpu.CompilerParams(collective_id=1, has_side_effects=True),
        name="finish",
    )(product, diag, part)


def body(glob_derivs, local_derivs, weights, residuals, track_ids, module_blocks, weak_modes):
    e = exchange(glob_derivs[0], local_derivs[0], weights[0], residuals[0], track_ids[0])
    schur, product, part, diag = place(module_blocks.T, weak_modes.T, *e)
    weak, tile, rhs = finish(product, diag, part)
    here = jnp.arange(GB)[:, None, None] == lax.axis_index("col")
    layer = jnp.where(here, tile[None], jnp.zeros((), f32)).reshape(GB * BW, BW)
    return schur, layer, rhs.reshape(GB * BW), weak.T


def solution(mesh):
    placed = (
        P(("row", "col"), None, None, None),
        P(("row", "col"), None, None, None),
        P(("row", "col"), None, None),
        P(("row", "col"), None, None),
        P(("row", "col"), None, None),
        P(),
        P("col", None),
    )
    return jax.shard_map(
        body,
        mesh=mesh,
        in_specs=placed,
        out_specs=(P("row", "col"), P("row", "col"), P("row"), P(("row", "col"), None)),
        check_vma=False,
    )
```

```python
import functools

import jax
import jax.numpy as jnp
from jax import lax
from jax.experimental import pallas as pl
from jax.experimental.pallas import tpu as pltpu
from jax.sharding import PartitionSpec as P

BW = 128
GB = 8
LOC = 4
TRK = 256
LAYERS = 16
PER = 256
ROWS = (88, 88, 80)
SIZE = {"y": 4, "z": 4, "X": 8}
ORDERS = (("y", "z", "X"), ("z", "X", "y"), ("X", "y", "z"))
RING = (1, 3, 2)
WIDE = (2, 6, 3, 7, 4, 5, 1)
UNROLL1 = 2
UNROLL2 = 2
CHUNKS = (2, 6, 3, 7, 0, 4, 5, 1)
MESH = pl.DeviceIdType.MESH
f32 = jnp.float32
bf16 = jnp.bfloat16


def split3(v):
    hi = v.astype(bf16)
    rest = v - hi.astype(f32)
    mid = rest.astype(bf16)
    low = (rest - mid.astype(f32)).astype(bf16)
    return hi, mid, low


def nt(a, b):
    return lax.dot_general(a, b, (((1,), (1,)), ((), ())), preferred_element_type=f32)


def nn(a, b):
    return lax.dot_general(a, b, (((1,), (0,)), ((), ())), preferred_element_type=f32)


def local_terms(glob, local, weight, resid, tracks, h_all, x_all, sums, q_ref, k_ref):
    sums[...] = jnp.zeros_like(sums)

    def first(s, carry):
        gt_low = jnp.transpose(glob[s].astype(f32)).astype(bf16)
        t = tracks[pl.ds(s, 1), :]
        w = weight[pl.ds(s, 1), :]
        r = resid[pl.ds(s, 1), :]
        hot = lax.broadcasted_iota(jnp.int32, (TRK, PER), 0) == t
        a = local[s]
        wa = w * a
        zero = jnp.zeros((), f32)
        row = pl.ds(pl.multiple_of(s * BW, BW), BW)
        for j in range(LOC):
            spread = jnp.where(hot, wa[j : j + 1, :], zero).astype(bf16)
            h_all[row, j * TRK : (j + 1) * TRK] = nt(gt_low, spread).astype(bf16)
        terms = []
        for i in range(LOC):
            terms.append(wa[i : i + 1, :] * a)
        terms.append(wa * r)
        terms.append(jnp.zeros((4, PER), f32))
        stacked = jnp.concatenate(terms, axis=0)
        hot_low = jnp.where(hot, jnp.ones((), f32), zero).astype(bf16)
        hi, mid, low = split3(stacked)
        sums[...] += nt(hi, hot_low) + nt(mid, hot_low) + nt(low, hot_low)
        return carry

    lax.fori_loop(0, LAYERS, first, 0, unroll=UNROLL1)

    one = jnp.ones((1, TRK), f32)
    nil = jnp.zeros((1, TRK), f32)
    rows = [
        [sums[4 * i + j : 4 * i + j + 1, :] + (one if i == j else nil) for j in range(LOC)]
        for i in range(LOC)
    ]
    inv = [[one if i == j else nil for j in range(LOC)] for i in range(LOC)]
    for p in range(LOC):
        pivot = rows[p][p]
        scaled = [v / pivot for v in rows[p]]
        scaled_inv = [v / pivot for v in inv[p]]
        for o in range(LOC):
            if o != p:
                factor = rows[o][p]
                rows[o] = [u - factor * v for u, v in zip(rows[o], scaled)]
                inv[o] = [u - factor * v for u, v in zip(inv[o], scaled_inv)]
        rows[p] = scaled
        inv[p] = scaled_inv
    for i in range(LOC):
        for j in range(LOC):
            k_ref[4 * i + j : 4 * i + j + 1, :] = inv[i][j]
    for j in range(LOC):
        q_ref[:, j * TRK : (j + 1) * TRK] = jnp.broadcast_to(
            sums[16 + j : 17 + j, :].astype(bf16), (16, TRK)
        )

    def second(s, carry):
        row = pl.ds(pl.multiple_of(s * BW, BW), BW)
        h = [h_all[row, l * TRK : (l + 1) * TRK].astype(f32) for l in range(LOC)]
        for j in range(LOC):
            x = h[0] * k_ref[j : j + 1, :]
            for l in range(1, LOC):
                x = x + h[l] * k_ref[4 * l + j : 4 * l + j + 1, :]
            x_all[row, j * TRK : (j + 1) * TRK] = (-x).astype(bf16)
        return carry

    lax.fori_loop(0, LAYERS, second, 0, unroll=UNROLL2)


def vectors(glob, weight, resid, x_all, q_ref, v_all):
    def term(s, carry):
        wr = (weight[pl.ds(s, 1), :] * resid[pl.ds(s, 1), :]).astype(bf16)
        x = x_all[pl.ds(pl.multiple_of(s * BW, BW), BW), :]
        both = nn(jnp.broadcast_to(wr, (16, PER)), glob[s]) + nt(q_ref[...], x)
        v_all[s // 4, s % 4] = both[:8]
        return carry

    lax.fori_loop(0, LAYERS, term, 0)


def tiles_for(c, start, stop, a0, a1, a2, h_all, x_all):
    right = h_all[pl.ds(pl.multiple_of(c * 2 * BW, 2 * BW), 2 * BW), :]

    def gram(y, carry):
        out = nt(x_all[pl.ds(pl.multiple_of(y * 4 * BW, 4 * BW), 4 * BW), :], right)
        for z in range(4):
            part = out[z * BW : (z + 1) * BW, :]
            a0[y, z, c] = part[0:88, :BW]
            a1[z, c, y, 0:40] = part[88:BW, :BW]
            a1[z, c, y, 40:88] = part[0:48, BW:]
            a2[c, y, z] = part[48:BW, BW:]
        return carry

    lax.fori_loop(start, stop, gram, 0)


def diagonal(c, glob, weight, a0, a1, a2):
    def own(s):
        g = glob[s]
        return nn((jnp.transpose(g.astype(f32)) * weight[pl.ds(s, 1), :]).astype(bf16), g)

    s = 2 * c
    y, z = s // 4, s % 4
    d = own(s)
    a0[y, z, c] += d[0:88]
    a1[z, c, y, 0:40] += d[88:BW]
    d = own(s + 1)
    a1[z + 1, c, y, 40:88] += d[0:48]
    a2[c, y, z + 1] += d[48:BW]


def coords():
    r, c = lax.axis_index("row"), lax.axis_index("col")
    return {"y": r // 4, "z": r % 4, "X": c}


def moved(me, dim, offset, sign):
    if dim == "X":
        x, k = me["X"] // 2, me["X"] % 2
        dx, dk = offset // 2, offset % 2
        return ((x + 4 + sign * dx) % 4) * 2 + (k + dk) % 2
    return (me[dim] + 4 + sign * offset) % 4


def device(me, dim, place):
    at = dict(me)
    at[dim] = place
    return (at["y"] * 4 + at["z"], at["X"])


def offsets(dim):
    return WIDE if dim == "X" else RING


def greet(me, dims):
    barrier = pltpu.get_barrier_semaphore()
    count = 0
    for dim in dims:
        for o in offsets(dim):
            pl.semaphore_signal(
                barrier,
                inc=1,
                device_id=device(me, dim, moved(me, dim, o, 1)),
                device_id_type=MESH,
            )
            count += 1
    return barrier, count


def exchange_kernel(glob, local, weight, resid, tracks, *refs):
    e, v_out, b, cc = refs[0:3], refs[3], refs[4:7], refs[7:10]
    a = refs[10:13]
    bounce2, bounce3 = refs[13:16], refs[16:19]
    h_all, x_all, v_all, v_mid, sums, q_ref, k_ref = refs[19:26]
    ssem, r1, r2, r3, into_sem, out_sem, v_sem = refs[26:33]
    me = coords()
    barrier, count = greet(me, ("y", "z", "X"))
    local_terms(glob, local, weight, resid, tracks, h_all, x_all, sums, q_ref, k_ref)
    pl.semaphore_wait(barrier, count)

    def send(src, dst, ssem, rsem, dim, place):
        cp = pltpu.make_async_remote_copy(
            src_ref=src,
            dst_ref=dst,
            send_sem=ssem,
            recv_sem=rsem,
            device_id=device(me, dim, place),
            device_id_type=MESH,
        )
        cp.start()

    def wait_for(ref, sem):
        pltpu.make_async_copy(ref, ref, sem).wait()

    pending = []

    def local_copy(src, mid, dst, sem):
        into = pltpu.make_async_copy(src, mid, into_sem)
        into.start()
        pending.append((into, pltpu.make_async_copy(mid, dst, sem)))

    def flush():
        for into, out in pending:
            into.wait()
            out.start()
        pending.clear()

    def stage1(j):
        o = CHUNKS[j]
        c = moved(me, "X", o, 1)
        for oo in RING:
            to = moved(me, "y", oo, 1)
            send(a[0].at[to, :, c], b[0].at[me["y"], :, c], ssem.at[0, 0], r1.at[0, oo], "y", to)
            to = moved(me, "z", oo, 1)
            send(a[1].at[to, c], b[1].at[me["z"], c], ssem.at[0, 1], r1.at[1, oo], "z", to)
        if o:
            send(a[2].at[c], b[2].at[me["X"]], ssem.at[0, 2], r1.at[2, o], "X", c)

    for j, o in enumerate(CHUNKS):
        c = moved(me, "X", o, 1)
        tiles_for(c, 0, 1, *a, h_all, x_all)
        if j:
            stage1(j - 1)
        tiles_for(c, 1, 4, *a, h_all, x_all)
        diagonal(c, glob, weight, *a)
    vectors(glob, weight, resid, x_all, q_ref, v_all)
    stage1(7)
    for oo in RING:
        to = moved(me, "y", oo, 1)
        send(v_all.at[to], v_mid.at[me["y"]], v_sem.at[0], v_sem.at[1], "y", to)
    v_mid[me["y"]] = v_all[me["y"]]

    for step in range(8):
        for g, order in enumerate(ORDERS):
            d1, d2, _ = order
            offs = (0,) + offsets(d1)
            if step >= len(offs):
                continue
            o1 = offs[step]
            src1 = moved(me, d1, o1, -1)
            if o1:
                wait_for(b[g].at[src1], r1.at[g, o1])
            for o2 in offsets(d2):
                to = moved(me, d2, o2, 1)
                src = b[g].at[src1, to] if o1 else a[g].at[me[d1], to]
                send(src, cc[g].at[me[d2], src1], ssem.at[1, g], r2.at[g, o2], d2, to)
            flush()
            back = cc[g].at[me[d2], src1]
            if o1:
                local_copy(b[g].at[src1, me[d2]], bounce2[g].at[o1], back, out_sem.at[0, g])
            else:
                pltpu.make_async_copy(a[g].at[me[d1], me[d2]], back, out_sem.at[0, g]).start()
    wait_for(v_mid.at[0:3], v_sem.at[1])
    for oo in RING:
        to = moved(me, "z", oo, 1)
        send(v_mid.at[:, to], v_out.at[me["z"]], v_sem.at[2], v_sem.at[3], "z", to)
    v_out[me["z"]] = v_mid[:, me["z"]]
    flush()
    for step in range(8):
        for g, order in enumerate(ORDERS):
            d1, d2, d3 = order
            offs = (0,) + offsets(d2)
            if step >= len(offs):
                continue
            o2 = offs[step]
            src2 = moved(me, d2, o2, -1)
            wait_for(cc[g].at[src2], r2.at[g, o2] if o2 else out_sem.at[0, g])
            for o3 in offsets(d3):
                to = moved(me, d3, o3, 1)
                send(
                    cc[g].at[src2, :, to],
                    e[g].at[me[d3], src2],
                    ssem.at[2, g],
                    r3.at[g],
                    d3,
                    to,
                )
            flush()
            local_copy(
                cc[g].at[src2, :, me[d3]],
                bounce3[g].at[o2],
                e[g].at[me[d3], src2],
                out_sem.at[1, g],
            )
    flush()
    wait_for(v_mid.at[0:3], v_sem.at[3])
    for g, order in enumerate(ORDERS):
        n1, n2, n3 = (SIZE[d] for d in order)
        wait_for(e[g].at[me[order[2]]], out_sem.at[1, g])
        wait_for(e[g].at[0 : n3 - 1], r3.at[g])
        wait_for(b[g].at[0 : n1 - 1], ssem.at[0, g])
        wait_for(cc[g].at[0 : n2 - 1], ssem.at[1, g])
        wait_for(e[g].at[0 : n3 - 1], ssem.at[2, g])
    wait_for(v_mid.at[0:3], v_sem.at[0])
    wait_for(v_mid.at[0:3], v_sem.at[2])


def exchange(glob, local, weight, resid, tracks):
    sizes = [tuple(SIZE[d] for d in order) for order in ORDERS]
    items = [(rows, BW) for rows in ROWS]
    both = list(zip(sizes, items))
    shapes = (
        [jax.ShapeDtypeStruct((n3, n2, n1) + it, f32) for (n1, n2, n3), it in both]
        + [jax.ShapeDtypeStruct((4, 4, 8, BW), f32)]
        + [jax.ShapeDtypeStruct((n1, n2, n3) + it, f32) for (n1, n2, n3), it in both]
        + [jax.ShapeDtypeStruct((n2, n1, n3) + it, f32) for (n1, n2, n3), it in both]
    )
    any_ = pl.BlockSpec(memory_space=pl.ANY)
    vmem = pl.BlockSpec(memory_space=pltpu.VMEM)
    out = pl.pallas_call(
        exchange_kernel,
        out_shape=tuple(shapes),
        in_specs=[vmem] * 5,
        out_specs=(any_,) * 3 + (vmem,) + (any_,) * 6,
        scratch_shapes=[pltpu.VMEM(n + it, f32) for n, it in both]
        + [pltpu.VMEM((n1, n3) + it, f32) for (n1, n2, n3), it in both]
        + [pltpu.VMEM((n2, n1) + it, f32) for (n1, n2, n3), it in both]
        + [
            pltpu.VMEM((LAYERS * BW, LOC * TRK), bf16),
            pltpu.VMEM((LAYERS * BW, LOC * TRK), bf16),
            pltpu.VMEM((4, 4, 8, BW), f32),
            pltpu.VMEM((4, 4, 8, BW), f32),
            pltpu.VMEM((24, TRK), f32),
            pltpu.VMEM((16, LOC * TRK), bf16),
            pltpu.VMEM((16, TRK), f32),
            pltpu.SemaphoreType.DMA((3, 3)),
            pltpu.SemaphoreType.DMA((3, 8)),
            pltpu.SemaphoreType.DMA((3, 8)),
            pltpu.SemaphoreType.DMA((3,)),
            pltpu.SemaphoreType.DMA,
            pltpu.SemaphoreType.DMA((2, 3)),
            pltpu.SemaphoreType.DMA((4,)),
        ],
        compiler_params=pltpu.CompilerParams(
            collective_id=0, has_side_effects=True, vmem_limit_bytes=60 << 20
        ),
        name="exchange",
    )(glob, local, weight, resid, tracks)
    return out[:4]


def place_kernel(
    blocks, weak, e0, e1, e2, vec, schur, product, rhs, diag, b0, b1, b2, acc, w_ref, p_ref, isem, sem
):
    row, col = lax.axis_index("row"), lax.axis_index("col")

    def fetch(i):
        return (
            pltpu.make_async_copy(e0.at[i], b0.at[i], isem.at[0, i]),
            pltpu.make_async_copy(e1.at[:, i], b1.at[:, i], isem.at[1, i]),
            pltpu.make_async_copy(e2.at[:, :, i], b2.at[:, :, i], isem.at[2, i]),
        )

    for i in range(8):
        for cp in fetch(i):
            cp.start()
    acc[...] = jnp.zeros_like(acc)
    rhs[...] = jnp.zeros_like(rhs)
    w = weak[...]
    w_hi = w.astype(bf16)
    w_ref[0:64, :] = w_hi
    w_ref[64:128, :] = (w - w_hi.astype(f32)).astype(bf16)
    p_ref[...] = jnp.zeros_like(p_ref)

    def term(i, carry):
        k = blocks[row, i * 8 + col]
        rhs[pl.ds(k, 1), :] += vec[i % 4, i // 4, 0:1]
        return carry

    lax.fori_loop(0, 16, term, 0)

    def batch(xb, carry):
        for cp in fetch(xb):
            cp.wait()

        def bundle(i, carry):
            y, z = i // 4, i % 4
            b = i * 8 + xb
            l0 = pl.multiple_of(blocks[2 * col, b] * BW, BW)
            l1 = pl.multiple_of(blocks[2 * col + 1, b] * BW + GB * BW, BW)
            r = pl.multiple_of(blocks[row, b] * BW, BW)
            acc[pl.ds(r, 88), pl.ds(l0, BW)] += b0[xb, z, y]
            acc[pl.ds(r + 88, 40), pl.ds(l0, BW)] += b1[y, xb, z, 0:40]
            acc[pl.ds(r, 48), pl.ds(l1, BW)] += b1[y, xb, z, 40:88]
            acc[pl.ds(r + 48, 80), pl.ds(l1, BW)] += b2[z, y, xb]
            return carry

        return lax.fori_loop(0, 16, bundle, carry)

    lax.fori_loop(0, 8, batch, 0)

    def copy_out(ch):
        cols = pl.ds(pl.multiple_of(ch * 256, 256), 256)
        return pltpu.make_async_copy(acc.at[:, cols], schur.at[:, cols], sem.at[ch])

    def chunk(ch, carry):
        cols = pl.ds(pl.multiple_of(ch * 256, 256), 256)
        wc = w_ref[:, cols]
        v = acc[:, cols]
        hi = v.astype(bf16)
        lo = (v - hi.astype(f32)).astype(bf16)
        p_ref[...] += nt(hi, wc) + nt(lo, wc)

        @pl.when(ch // 4 == row % 2)
        def _():
            for m in range(2):
                k = 2 * (ch % 4) + m
                diag[k] = acc[
                    pl.ds(pl.multiple_of(k * BW, BW), BW),
                    pl.ds(pl.multiple_of(ch * 256 + m * BW, BW), BW),
                ]

            @pl.when(col == row // 2)
            def _():
                acc[:, cols] = jnp.zeros((GB * BW, 256), f32)

        copy_out(ch).start()
        return carry

    lax.fori_loop(0, 8, chunk, 0)
    for k in range(GB):
        pt = jnp.transpose(p_ref[k * BW : (k + 1) * BW, :])
        product[k] = pt[0:64] + pt[64:128]
    for ch in range(8):
        copy_out(ch).wait()


def place(blocks, weak, e0, e1, e2, vec):
    vmem = pl.BlockSpec(memory_space=pltpu.VMEM)
    any_ = pl.BlockSpec(memory_space=pl.ANY)
    return pl.pallas_call(
        place_kernel,
        in_specs=[pl.BlockSpec(memory_space=pltpu.SMEM), vmem, any_, any_, any_, vmem],
        out_specs=(any_, vmem, vmem, vmem),
        out_shape=(
            jax.ShapeDtypeStruct((GB * BW, 2 * GB * BW), f32),
            jax.ShapeDtypeStruct((GB, 64, BW), f32),
            jax.ShapeDtypeStruct((GB, BW), f32),
            jax.ShapeDtypeStruct((GB, BW, BW), f32),
        ),
        scratch_shapes=[
            pltpu.VMEM(e0.shape, f32),
            pltpu.VMEM(e1.shape, f32),
            pltpu.VMEM(e2.shape, f32),
            pltpu.VMEM((GB * BW, 2 * GB * BW), f32),
            pltpu.VMEM((BW, 2 * GB * BW), bf16),
            pltpu.VMEM((GB * BW, BW), f32),
            pltpu.SemaphoreType.DMA((3, 8)),
            pltpu.SemaphoreType.DMA((8,)),
        ],
        compiler_params=pltpu.CompilerParams(vmem_limit_bytes=56 << 20),
        name="place",
    )(blocks, weak, e0, e1, e2, vec)


def finish_kernel(product, diag, part, weak, tile, rhs, got, got_r, ssem, rsem):
    me = coords()
    row = lax.axis_index("row")
    mine = me["X"]
    owner = row // 2
    barrier, count = greet(me, ("X",))
    pl.semaphore_wait(barrier, count)

    def copy(src, dst, i, to):
        return pltpu.make_async_remote_copy(
            src_ref=src,
            dst_ref=dst,
            send_sem=ssem.at[i],
            recv_sem=rsem.at[i],
            device_id=device(me, "X", to),
            device_id_type=MESH,
        )

    def wait_for(ref, sem):
        pltpu.make_async_copy(ref, ref, sem).wait()

    for o in WIDE:
        to = moved(me, "X", o, 1)
        copy(product.at[to], got.at[o - 1], 0, to).start()
        copy(part, got_r.at[o - 1], 1, to).start()

    @pl.when(mine == owner)
    def _():
        for o in WIDE:
            to = moved(me, "X", o, 1)
            copy(diag.at[to], tile, 2, to).start()
        tile[...] = diag[mine]

    wait_for(got, rsem.at[0])
    wait_for(got_r, rsem.at[1])
    total = product[mine]
    total_r = part[...]
    for o in range(7):
        total = total + got[o]
        total_r = total_r + got_r[o]
    weak[...] = total
    rhs[...] = total_r
    wait_for(got, ssem.at[0])
    wait_for(got_r, ssem.at[1])

    @pl.when(mine != owner)
    def _():
        wait_for(tile, rsem.at[2])

    @pl.when(mine == owner)
    def _():
        wait_for(diag.at[0:7], ssem.at[2])


def finish(product, diag, part):
    vmem = pl.BlockSpec(memory_space=pltpu.VMEM)
    return pl.pallas_call(
        finish_kernel,
        out_shape=(
            jax.ShapeDtypeStruct((64, BW), f32),
            jax.ShapeDtypeStruct((BW, BW), f32),
            jax.ShapeDtypeStruct((GB, BW), f32),
        ),
        in_specs=[vmem] * 3,
        out_specs=(vmem,) * 3,
        scratch_shapes=[
            pltpu.VMEM((7, 64, BW), f32),
            pltpu.VMEM((7, GB, BW), f32),
            pltpu.SemaphoreType.DMA((3,)),
            pltpu.SemaphoreType.DMA((3,)),
        ],
        compiler_params=pltpu.CompilerParams(collective_id=1, has_side_effects=True),
        name="finish",
    )(product, diag, part)


def emit_kernel(weak_in, tile, rhs_in, weak, layer, rhs):
    col = lax.axis_index("col")
    weak[...] = weak_in[...]
    rhs[...] = rhs_in[...]
    layer[...] = jnp.zeros_like(layer)
    layer[pl.ds(pl.multiple_of(col * BW, BW), BW), :] = tile[...]


def emit(weak, tile, rhs):
    vmem = pl.BlockSpec(memory_space=pltpu.VMEM)
    return pl.pallas_call(
        emit_kernel,
        out_shape=(
            jax.ShapeDtypeStruct((64, BW), f32),
            jax.ShapeDtypeStruct((GB * BW, BW), f32),
            jax.ShapeDtypeStruct((GB, BW), f32),
        ),
        in_specs=[vmem] * 3,
        out_specs=(vmem,) * 3,
        name="emit",
    )(weak, tile, rhs)


def body(glob_derivs, local_derivs, weights, residuals, track_ids, module_blocks, weak_modes):
    e = exchange(glob_derivs[0], local_derivs[0], weights[0], residuals[0], track_ids[0])
    schur, product, part, diag = place(module_blocks.T, weak_modes.T, *e)
    weak, layer, rhs = emit(*finish(product, diag, part))
    return schur, layer, rhs.reshape(GB * BW), weak.T


def solution(mesh):
    placed = (
        P(("row", "col"), None, None, None),
        P(("row", "col"), None, None, None),
        P(("row", "col"), None, None),
        P(("row", "col"), None, None),
        P(("row", "col"), None, None),
        P(),
        P("col", None),
    )
    return jax.shard_map(
        body,
        mesh=mesh,
        in_specs=placed,
        out_specs=(P("row", "col"), P("row", "col"), P("row"), P(("row", "col"), None)),
        check_vma=False,
    )
```

```python
import functools

import jax
import jax.numpy as jnp
from jax import lax
from jax.experimental import pallas as pl
from jax.experimental.pallas import tpu as pltpu
from jax.sharding import PartitionSpec as P

BW = 128
GB = 8
LOC = 4
TRK = 256
LAYERS = 16
PER = 256
ROWS = (88, 88, 80)
SIZE = {"y": 4, "z": 4, "X": 8}
ORDERS = (("y", "z", "X"), ("z", "X", "y"), ("X", "y", "z"))
RING = (1, 3, 2)
WIDE = (2, 6, 3, 7, 4, 5, 1)
UNROLL1 = 2
UNROLL2 = 2
CHUNKS = (2, 6, 3, 7, 0, 4, 5, 1)
MESH = pl.DeviceIdType.MESH
f32 = jnp.float32
bf16 = jnp.bfloat16


def split3(v):
    hi = v.astype(bf16)
    rest = v - hi.astype(f32)
    mid = rest.astype(bf16)
    low = (rest - mid.astype(f32)).astype(bf16)
    return hi, mid, low


def nt(a, b):
    return lax.dot_general(a, b, (((1,), (1,)), ((), ())), preferred_element_type=f32)


def nn(a, b):
    return lax.dot_general(a, b, (((1,), (0,)), ((), ())), preferred_element_type=f32)


def local_terms(glob, local, weight, resid, tracks, h_all, x_all, sums, q_ref, k_ref):
    sums[...] = jnp.zeros_like(sums)

    def first(s, carry):
        gt_low = jnp.transpose(glob[s].astype(f32)).astype(bf16)
        t = tracks[pl.ds(s, 1), :]
        w = weight[pl.ds(s, 1), :]
        r = resid[pl.ds(s, 1), :]
        hot = lax.broadcasted_iota(jnp.int32, (TRK, PER), 0) == t
        a = local[s]
        wa = w * a
        zero = jnp.zeros((), f32)
        row = pl.ds(pl.multiple_of(s * BW, BW), BW)
        for j in range(LOC):
            spread = jnp.where(hot, wa[j : j + 1, :], zero).astype(bf16)
            h_all[row, j * TRK : (j + 1) * TRK] = nt(gt_low, spread).astype(bf16)
        terms = []
        for i in range(LOC):
            terms.append(wa[i : i + 1, :] * a)
        terms.append(wa * r)
        terms.append(jnp.zeros((4, PER), f32))
        stacked = jnp.concatenate(terms, axis=0)
        hot_low = jnp.where(hot, jnp.ones((), f32), zero).astype(bf16)
        hi, mid, low = split3(stacked)
        sums[...] += nt(hi, hot_low) + nt(mid, hot_low) + nt(low, hot_low)
        return carry

    lax.fori_loop(0, LAYERS, first, 0, unroll=UNROLL1)

    one = jnp.ones((1, TRK), f32)
    nil = jnp.zeros((1, TRK), f32)
    rows = [
        [sums[4 * i + j : 4 * i + j + 1, :] + (one if i == j else nil) for j in range(LOC)]
        for i in range(LOC)
    ]
    inv = [[one if i == j else nil for j in range(LOC)] for i in range(LOC)]
    for p in range(LOC):
        pivot = rows[p][p]
        scaled = [v / pivot for v in rows[p]]
        scaled_inv = [v / pivot for v in inv[p]]
        for o in range(LOC):
            if o != p:
                factor = rows[o][p]
                rows[o] = [u - factor * v for u, v in zip(rows[o], scaled)]
                inv[o] = [u - factor * v for u, v in zip(inv[o], scaled_inv)]
        rows[p] = scaled
        inv[p] = scaled_inv
    for i in range(LOC):
        for j in range(LOC):
            k_ref[4 * i + j : 4 * i + j + 1, :] = inv[i][j]
    for j in range(LOC):
        q_ref[:, j * TRK : (j + 1) * TRK] = jnp.broadcast_to(
            sums[16 + j : 17 + j, :].astype(bf16), (16, TRK)
        )

    def second(s, carry):
        row = pl.ds(pl.multiple_of(s * BW, BW), BW)
        h = [h_all[row, l * TRK : (l + 1) * TRK].astype(f32) for l in range(LOC)]
        for j in range(LOC):
            x = h[0] * k_ref[j : j + 1, :]
            for l in range(1, LOC):
                x = x + h[l] * k_ref[4 * l + j : 4 * l + j + 1, :]
            x_all[row, j * TRK : (j + 1) * TRK] = (-x).astype(bf16)
        return carry

    lax.fori_loop(0, LAYERS, second, 0, unroll=UNROLL2)


def vectors(glob, weight, resid, x_all, q_ref, v_all):
    def term(s, carry):
        wr = (weight[pl.ds(s, 1), :] * resid[pl.ds(s, 1), :]).astype(bf16)
        x = x_all[pl.ds(pl.multiple_of(s * BW, BW), BW), :]
        both = nn(jnp.broadcast_to(wr, (16, PER)), glob[s]) + nt(q_ref[...], x)
        v_all[s // 4, s % 4] = both[:8]
        return carry

    lax.fori_loop(0, LAYERS, term, 0)


def tiles_for(c, start, stop, a0, a1, a2, h_all, x_all):
    right = h_all[pl.ds(pl.multiple_of(c * 2 * BW, 2 * BW), 2 * BW), :]

    def gram(y, carry):
        out = nt(x_all[pl.ds(pl.multiple_of(y * 4 * BW, 4 * BW), 4 * BW), :], right)
        for z in range(4):
            part = out[z * BW : (z + 1) * BW, :]
            a0[y, z, c] = part[0:88, :BW]
            a1[z, c, y, 0:40] = part[88:BW, :BW]
            a1[z, c, y, 40:88] = part[0:48, BW:]
            a2[c, y, z] = part[48:BW, BW:]
        return carry

    lax.fori_loop(start, stop, gram, 0)


def diagonal(c, glob, weight, a0, a1, a2):
    def own(s):
        g = glob[s]
        return nn((jnp.transpose(g.astype(f32)) * weight[pl.ds(s, 1), :]).astype(bf16), g)

    s = 2 * c
    y, z = s // 4, s % 4
    d = own(s)
    a0[y, z, c] += d[0:88]
    a1[z, c, y, 0:40] += d[88:BW]
    d = own(s + 1)
    a1[z + 1, c, y, 40:88] += d[0:48]
    a2[c, y, z + 1] += d[48:BW]


def coords():
    r, c = lax.axis_index("row"), lax.axis_index("col")
    return {"y": r // 4, "z": r % 4, "X": c}


def moved(me, dim, offset, sign):
    if dim == "X":
        x, k = me["X"] // 2, me["X"] % 2
        dx, dk = offset // 2, offset % 2
        return ((x + 4 + sign * dx) % 4) * 2 + (k + dk) % 2
    return (me[dim] + 4 + sign * offset) % 4


def device(me, dim, place):
    at = dict(me)
    at[dim] = place
    return (at["y"] * 4 + at["z"], at["X"])


def offsets(dim):
    return WIDE if dim == "X" else RING


def greet(me, dims):
    barrier = pltpu.get_barrier_semaphore()
    count = 0
    for dim in dims:
        for o in offsets(dim):
            pl.semaphore_signal(
                barrier,
                inc=1,
                device_id=device(me, dim, moved(me, dim, o, 1)),
                device_id_type=MESH,
            )
            count += 1
    return barrier, count


def exchange_kernel(*refs):
    given, refs = refs[:5], refs[5:]
    e, v_out, b, cc = refs[0:3], refs[3], refs[4:7], refs[7:10]
    a = refs[10:13]
    bounce2 = refs[13:16]
    h_all, x_all, v_all, v_mid, sums, q_ref, k_ref = refs[16:23]
    ssem, r1, r2, r3, into_sem, out_sem, v_sem = refs[23:30]
    glob, local, weight, resid, tracks, in_sem = refs[30:36]
    loads = [
        pltpu.make_async_copy(src, dst, in_sem.at[i])
        for i, (src, dst) in enumerate(zip(given, (glob, local, weight, resid, tracks)))
    ]
    for cp in loads:
        cp.start()
    me = coords()
    barrier, count = greet(me, ("y", "z", "X"))
    for cp in loads:
        cp.wait()
    local_terms(glob, local, weight, resid, tracks, h_all, x_all, sums, q_ref, k_ref)
    pl.semaphore_wait(barrier, count)

    def send(src, dst, ssem, rsem, dim, place):
        cp = pltpu.make_async_remote_copy(
            src_ref=src,
            dst_ref=dst,
            send_sem=ssem,
            recv_sem=rsem,
            device_id=device(me, dim, place),
            device_id_type=MESH,
        )
        cp.start()

    def wait_for(ref, sem):
        pltpu.make_async_copy(ref, ref, sem).wait()

    pending = []

    def local_copy(src, mid, dst, sem):
        into = pltpu.make_async_copy(src, mid, into_sem)
        into.start()
        pending.append((into, pltpu.make_async_copy(mid, dst, sem)))

    def flush():
        for into, out in pending:
            into.wait()
            out.start()
        pending.clear()

    def stage1(j):
        o = CHUNKS[j]
        c = moved(me, "X", o, 1)
        for oo in RING:
            to = moved(me, "y", oo, 1)
            send(a[0].at[to, :, c], b[0].at[me["y"], :, c], ssem.at[0, 0], r1.at[0, oo], "y", to)
            to = moved(me, "z", oo, 1)
            send(a[1].at[to, c], b[1].at[me["z"], c], ssem.at[0, 1], r1.at[1, oo], "z", to)
        if o:
            send(a[2].at[c], b[2].at[me["X"]], ssem.at[0, 2], r1.at[2, o], "X", c)

    for j, o in enumerate(CHUNKS):
        c = moved(me, "X", o, 1)
        tiles_for(c, 0, 1, *a, h_all, x_all)
        if j:
            stage1(j - 1)
        tiles_for(c, 1, 4, *a, h_all, x_all)
        diagonal(c, glob, weight, *a)
    vectors(glob, weight, resid, x_all, q_ref, v_all)
    stage1(7)
    for oo in RING:
        to = moved(me, "y", oo, 1)
        send(v_all.at[to], v_mid.at[me["y"]], v_sem.at[0], v_sem.at[1], "y", to)
    v_mid[me["y"]] = v_all[me["y"]]

    for step in range(8):
        for g, order in enumerate(ORDERS):
            d1, d2, _ = order
            offs = (0,) + offsets(d1)
            if step >= len(offs):
                continue
            o1 = offs[step]
            src1 = moved(me, d1, o1, -1)
            if o1:
                wait_for(b[g].at[src1], r1.at[g, o1])
            for o2 in offsets(d2):
                to = moved(me, d2, o2, 1)
                src = b[g].at[src1, to] if o1 else a[g].at[me[d1], to]
                send(src, cc[g].at[me[d2], src1], ssem.at[1, g], r2.at[g, o2], d2, to)
            flush()
            back = cc[g].at[me[d2], src1]
            if o1:
                local_copy(b[g].at[src1, me[d2]], bounce2[g].at[o1], back, out_sem.at[0, g])
            else:
                pltpu.make_async_copy(a[g].at[me[d1], me[d2]], back, out_sem.at[0, g]).start()
    wait_for(v_mid.at[0:3], v_sem.at[1])
    for oo in RING:
        to = moved(me, "z", oo, 1)
        send(v_mid.at[:, to], v_out.at[me["z"]], v_sem.at[2], v_sem.at[3], "z", to)
    v_out[me["z"]] = v_mid[:, me["z"]]
    flush()
    for step in range(8):
        for g, order in enumerate(ORDERS):
            d1, d2, d3 = order
            offs = (0,) + offsets(d2)
            if step >= len(offs):
                continue
            o2 = offs[step]
            src2 = moved(me, d2, o2, -1)
            wait_for(cc[g].at[src2], r2.at[g, o2] if o2 else out_sem.at[0, g])
            for o3 in offsets(d3):
                to = moved(me, d3, o3, 1)
                send(
                    cc[g].at[src2, :, to],
                    e[g].at[me[d3], src2],
                    ssem.at[2, g],
                    r3.at[g],
                    d3,
                    to,
                )
            pltpu.make_async_copy(
                cc[g].at[src2, :, me[d3]], e[g].at[me[d3], src2], out_sem.at[1, g]
            ).start()
    wait_for(v_mid.at[0:3], v_sem.at[3])
    for g, order in enumerate(ORDERS):
        n1, n2, n3 = (SIZE[d] for d in order)
        wait_for(e[g].at[me[order[2]]], out_sem.at[1, g])
        wait_for(e[g].at[0 : n3 - 1], r3.at[g])
        wait_for(b[g].at[0 : n1 - 1], ssem.at[0, g])
        wait_for(cc[g].at[0 : n2 - 1], ssem.at[1, g])
        wait_for(e[g].at[0 : n3 - 1], ssem.at[2, g])
    wait_for(v_mid.at[0:3], v_sem.at[0])
    wait_for(v_mid.at[0:3], v_sem.at[2])


def exchange(glob, local, weight, resid, tracks):
    sizes = [tuple(SIZE[d] for d in order) for order in ORDERS]
    items = [(rows, BW) for rows in ROWS]
    both = list(zip(sizes, items))
    shapes = (
        [pltpu.VMEM((n3, n2, n1) + it, f32) for (n1, n2, n3), it in both]
        + [jax.ShapeDtypeStruct((4, 4, 8, BW), f32)]
        + [jax.ShapeDtypeStruct((n1, n2, n3) + it, f32) for (n1, n2, n3), it in both]
        + [jax.ShapeDtypeStruct((n2, n1, n3) + it, f32) for (n1, n2, n3), it in both]
    )
    any_ = pl.BlockSpec(memory_space=pl.ANY)
    vmem = pl.BlockSpec(memory_space=pltpu.VMEM)
    out = pl.pallas_call(
        exchange_kernel,
        out_shape=tuple(shapes),
        in_specs=[pl.BlockSpec(memory_space=pltpu.HBM)] * 5,
        out_specs=(vmem,) * 3 + (vmem,) + (any_,) * 6,
        scratch_shapes=[pltpu.VMEM(n + it, f32) for n, it in both]
        + [pltpu.VMEM((n1, n3) + it, f32) for (n1, n2, n3), it in both]
        + [
            pltpu.VMEM((LAYERS * BW, LOC * TRK), bf16),
            pltpu.VMEM((LAYERS * BW, LOC * TRK), bf16),
            pltpu.VMEM((4, 4, 8, BW), f32),
            pltpu.VMEM((4, 4, 8, BW), f32),
            pltpu.VMEM((24, TRK), f32),
            pltpu.VMEM((16, LOC * TRK), bf16),
            pltpu.VMEM((16, TRK), f32),
            pltpu.SemaphoreType.DMA((3, 3)),
            pltpu.SemaphoreType.DMA((3, 8)),
            pltpu.SemaphoreType.DMA((3, 8)),
            pltpu.SemaphoreType.DMA((3,)),
            pltpu.SemaphoreType.DMA,
            pltpu.SemaphoreType.DMA((2, 3)),
            pltpu.SemaphoreType.DMA((4,)),
            pltpu.VMEM(glob.shape, bf16),
            pltpu.VMEM(local.shape, f32),
            pltpu.VMEM(weight.shape, f32),
            pltpu.VMEM(resid.shape, f32),
            pltpu.VMEM(tracks.shape, jnp.int32),
            pltpu.SemaphoreType.DMA((5,)),
        ],
        compiler_params=pltpu.CompilerParams(
            collective_id=0, has_side_effects=True, vmem_limit_bytes=36 << 20
        ),
        name="exchange",
    )(glob, local, weight, resid, tracks)
    return out[:4]


def place_kernel(
    given_b, given_w, e0, e1, e2, vec, schur, product, rhs, diag, acc, w_ref, p_ref, blocks, weak, sem, lsem
):
    row, col = lax.axis_index("row"), lax.axis_index("col")

    load_b = pltpu.make_async_copy(given_b, blocks, lsem.at[0])
    load_w = pltpu.make_async_copy(given_w, weak, lsem.at[1])
    load_b.start()
    load_w.start()
    acc[...] = jnp.zeros_like(acc)
    rhs[...] = jnp.zeros_like(rhs)
    load_w.wait()
    load_b.wait()
    w = weak[...]
    w_hi = w.astype(bf16)
    w_ref[0:64, :] = w_hi
    w_ref[64:128, :] = (w - w_hi.astype(f32)).astype(bf16)
    p_ref[...] = jnp.zeros_like(p_ref)

    def term(i, carry):
        k = blocks[row, i * 8 + col]
        rhs[pl.ds(k, 1), :] += vec[i % 4, i // 4, 0:1]
        return carry

    lax.fori_loop(0, 16, term, 0)

    def batch(xb, carry):
        def bundle(i, carry):
            y, z = i // 4, i % 4
            b = i * 8 + xb
            l0 = pl.multiple_of(blocks[2 * col, b] * BW, BW)
            l1 = pl.multiple_of(blocks[2 * col + 1, b] * BW + GB * BW, BW)
            r = pl.multiple_of(blocks[row, b] * BW, BW)
            acc[pl.ds(r, 88), pl.ds(l0, BW)] += e0[xb, z, y]
            acc[pl.ds(r + 88, 40), pl.ds(l0, BW)] += e1[y, xb, z, 0:40]
            acc[pl.ds(r, 48), pl.ds(l1, BW)] += e1[y, xb, z, 40:88]
            acc[pl.ds(r + 48, 80), pl.ds(l1, BW)] += e2[z, y, xb]
            return carry

        return lax.fori_loop(0, 16, bundle, carry)

    lax.fori_loop(0, 8, batch, 0)

    def copy_out(ch):
        cols = pl.ds(pl.multiple_of(ch * 256, 256), 256)
        return pltpu.make_async_copy(acc.at[:, cols], schur.at[:, cols], sem.at[ch])

    def chunk(ch, carry):
        cols = pl.ds(pl.multiple_of(ch * 256, 256), 256)
        wc = w_ref[:, cols]
        v = acc[:, cols]
        hi = v.astype(bf16)
        lo = (v - hi.astype(f32)).astype(bf16)
        p_ref[...] += nt(hi, wc) + nt(lo, wc)

        @pl.when(ch // 4 == row % 2)
        def _():
            for m in range(2):
                k = 2 * (ch % 4) + m
                diag[k] = acc[
                    pl.ds(pl.multiple_of(k * BW, BW), BW),
                    pl.ds(pl.multiple_of(ch * 256 + m * BW, BW), BW),
                ]

            @pl.when(col == row // 2)
            def _():
                acc[:, cols] = jnp.zeros((GB * BW, 256), f32)

        copy_out(ch).start()
        return carry

    lax.fori_loop(0, 8, chunk, 0)
    for k in range(GB):
        pt = jnp.transpose(p_ref[k * BW : (k + 1) * BW, :])
        product[k] = pt[0:64] + pt[64:128]
    for ch in range(8):
        copy_out(ch).wait()


def place(blocks, weak, e0, e1, e2, vec):
    vmem = pl.BlockSpec(memory_space=pltpu.VMEM)
    any_ = pl.BlockSpec(memory_space=pl.ANY)
    hbm = pl.BlockSpec(memory_space=pltpu.HBM)
    return pl.pallas_call(
        place_kernel,
        in_specs=[hbm, hbm, vmem, vmem, vmem, vmem],
        out_specs=(any_, vmem, vmem, vmem),
        out_shape=(
            jax.ShapeDtypeStruct((GB * BW, 2 * GB * BW), f32),
            jax.ShapeDtypeStruct((GB, 64, BW), f32),
            jax.ShapeDtypeStruct((GB, BW), f32),
            jax.ShapeDtypeStruct((GB, BW, BW), f32),
        ),
        scratch_shapes=[
            pltpu.VMEM((GB * BW, 2 * GB * BW), f32),
            pltpu.VMEM((BW, 2 * GB * BW), bf16),
            pltpu.VMEM((GB * BW, BW), f32),
            pltpu.SMEM(blocks.shape, jnp.int32),
            pltpu.VMEM(weak.shape, f32),
            pltpu.SemaphoreType.DMA((8,)),
            pltpu.SemaphoreType.DMA((2,)),
        ],
        compiler_params=pltpu.CompilerParams(vmem_limit_bytes=20 << 20),
        name="place",
    )(blocks, weak, e0, e1, e2, vec)


def finish_kernel(product, diag, part, weak, tile, rhs, got, got_r, ssem, rsem):
    me = coords()
    row = lax.axis_index("row")
    mine = me["X"]
    owner = row // 2
    barrier, count = greet(me, ("X",))
    pl.semaphore_wait(barrier, count)

    def copy(src, dst, i, to):
        return pltpu.make_async_remote_copy(
            src_ref=src,
            dst_ref=dst,
            send_sem=ssem.at[i],
            recv_sem=rsem.at[i],
            device_id=device(me, "X", to),
            device_id_type=MESH,
        )

    def wait_for(ref, sem):
        pltpu.make_async_copy(ref, ref, sem).wait()

    for o in WIDE:
        to = moved(me, "X", o, 1)
        copy(product.at[to], got.at[o - 1], 0, to).start()
        copy(part, got_r.at[o - 1], 1, to).start()

    @pl.when(mine == owner)
    def _():
        for o in WIDE:
            to = moved(me, "X", o, 1)
            copy(diag.at[to], tile, 2, to).start()
        tile[...] = diag[mine]

    wait_for(got, rsem.at[0])
    wait_for(got_r, rsem.at[1])
    total = product[mine]
    total_r = part[...]
    for o in range(7):
        total = total + got[o]
        total_r = total_r + got_r[o]
    weak[...] = total
    rhs[...] = total_r
    wait_for(got, ssem.at[0])
    wait_for(got_r, ssem.at[1])

    @pl.when(mine != owner)
    def _():
        wait_for(tile, rsem.at[2])

    @pl.when(mine == owner)
    def _():
        wait_for(diag.at[0:7], ssem.at[2])


def finish(product, diag, part):
    vmem = pl.BlockSpec(memory_space=pltpu.VMEM)
    return pl.pallas_call(
        finish_kernel,
        out_shape=(
            jax.ShapeDtypeStruct((64, BW), f32),
            jax.ShapeDtypeStruct((BW, BW), f32),
            jax.ShapeDtypeStruct((GB, BW), f32),
        ),
        in_specs=[vmem] * 3,
        out_specs=(vmem,) * 3,
        scratch_shapes=[
            pltpu.VMEM((7, 64, BW), f32),
            pltpu.VMEM((7, GB, BW), f32),
            pltpu.SemaphoreType.DMA((3,)),
            pltpu.SemaphoreType.DMA((3,)),
        ],
        compiler_params=pltpu.CompilerParams(
            collective_id=1, has_side_effects=True, vmem_limit_bytes=8 << 20
        ),
        name="finish",
    )(product, diag, part)


def emit_kernel(weak_in, tile, rhs_in, weak, layer, rhs):
    col = lax.axis_index("col")
    weak[...] = weak_in[...]
    rhs[...] = rhs_in[...]
    layer[...] = jnp.zeros_like(layer)
    layer[pl.ds(pl.multiple_of(col * BW, BW), BW), :] = tile[...]


def emit(weak, tile, rhs):
    vmem = pl.BlockSpec(memory_space=pltpu.VMEM)
    return pl.pallas_call(
        emit_kernel,
        out_shape=(
            jax.ShapeDtypeStruct((64, BW), f32),
            jax.ShapeDtypeStruct((GB * BW, BW), f32),
            jax.ShapeDtypeStruct((GB, BW), f32),
        ),
        in_specs=[vmem] * 3,
        out_specs=(vmem,) * 3,
        compiler_params=pltpu.CompilerParams(vmem_limit_bytes=8 << 20),
        name="emit",
    )(weak, tile, rhs)


def body(glob_derivs, local_derivs, weights, residuals, track_ids, module_blocks, weak_modes):
    def stay(v):
        return pltpu.with_memory_space_constraint(v, pltpu.HBM)

    inputs = (glob_derivs, local_derivs, weights, residuals, track_ids)
    e = exchange(*[stay(v[0]) for v in inputs])
    schur, product, part, diag = place(stay(module_blocks.T), stay(weak_modes.T), *e)
    weak, layer, rhs = emit(*finish(product, diag, part))
    return schur, layer, rhs.reshape(GB * BW), weak.T


def solution(mesh):
    placed = (
        P(("row", "col"), None, None, None),
        P(("row", "col"), None, None, None),
        P(("row", "col"), None, None),
        P(("row", "col"), None, None),
        P(("row", "col"), None, None),
        P(),
        P("col", None),
    )
    return jax.shard_map(
        body,
        mesh=mesh,
        in_specs=placed,
        out_specs=(P("row", "col"), P("row", "col"), P("row"), P(("row", "col"), None)),
        check_vma=False,
    )
```

```python
import functools

import jax
import jax.numpy as jnp
from jax import lax
from jax.experimental import pallas as pl
from jax.experimental.pallas import tpu as pltpu
from jax.sharding import PartitionSpec as P

BW = 128
GB = 8
LOC = 4
TRK = 256
LAYERS = 16
PER = 256
ROWS = (88, 88, 80)
SIZE = {"y": 4, "z": 4, "X": 8}
ORDERS = (("y", "z", "X"), ("z", "X", "y"), ("X", "y", "z"))
RING = (1, 3, 2)
WIDE = (2, 6, 3, 7, 4, 5, 1)
UNROLL1 = 4
UNROLL2 = 4
CHUNKS = (2, 6, 3, 7, 0, 4, 5, 1)
MESH = pl.DeviceIdType.MESH
f32 = jnp.float32
bf16 = jnp.bfloat16


def split3(v):
    hi = v.astype(bf16)
    rest = v - hi.astype(f32)
    mid = rest.astype(bf16)
    low = (rest - mid.astype(f32)).astype(bf16)
    return hi, mid, low


def nt(a, b):
    return lax.dot_general(a, b, (((1,), (1,)), ((), ())), preferred_element_type=f32)


def nn(a, b):
    return lax.dot_general(a, b, (((1,), (0,)), ((), ())), preferred_element_type=f32)


def local_terms(glob, local, weight, resid, tracks, h_all, x_all, sums, q_ref, k_ref):
    sums[...] = jnp.zeros_like(sums)

    def first(s, carry):
        gt_low = jnp.transpose(glob[s].astype(f32)).astype(bf16)
        t = tracks[pl.ds(s, 1), :]
        w = weight[pl.ds(s, 1), :]
        r = resid[pl.ds(s, 1), :]
        hot = lax.broadcasted_iota(jnp.int32, (TRK, PER), 0) == t
        a = local[s]
        wa = w * a
        zero = jnp.zeros((), f32)
        row = pl.ds(pl.multiple_of(s * BW, BW), BW)
        for j in range(LOC):
            spread = jnp.where(hot, wa[j : j + 1, :], zero).astype(bf16)
            h_all[row, j * TRK : (j + 1) * TRK] = nt(gt_low, spread).astype(bf16)
        terms = []
        for i in range(LOC):
            terms.append(wa[i : i + 1, :] * a)
        terms.append(wa * r)
        terms.append(jnp.zeros((4, PER), f32))
        stacked = jnp.concatenate(terms, axis=0)
        hot_low = jnp.where(hot, jnp.ones((), f32), zero).astype(bf16)
        hi, mid, low = split3(stacked)
        sums[...] += nt(hi, hot_low) + nt(mid, hot_low) + nt(low, hot_low)
        return carry

    lax.fori_loop(0, LAYERS, first, 0, unroll=UNROLL1)

    one = jnp.ones((1, TRK), f32)
    nil = jnp.zeros((1, TRK), f32)
    rows = [
        [sums[4 * i + j : 4 * i + j + 1, :] + (one if i == j else nil) for j in range(LOC)]
        for i in range(LOC)
    ]
    inv = [[one if i == j else nil for j in range(LOC)] for i in range(LOC)]
    for p in range(LOC):
        pivot = rows[p][p]
        scaled = [v / pivot for v in rows[p]]
        scaled_inv = [v / pivot for v in inv[p]]
        for o in range(LOC):
            if o != p:
                factor = rows[o][p]
                rows[o] = [u - factor * v for u, v in zip(rows[o], scaled)]
                inv[o] = [u - factor * v for u, v in zip(inv[o], scaled_inv)]
        rows[p] = scaled
        inv[p] = scaled_inv
    for i in range(LOC):
        for j in range(LOC):
            k_ref[4 * i + j : 4 * i + j + 1, :] = inv[i][j]
    for j in range(LOC):
        q_ref[:, j * TRK : (j + 1) * TRK] = jnp.broadcast_to(
            sums[16 + j : 17 + j, :].astype(bf16), (16, TRK)
        )

    def second(s, carry):
        row = pl.ds(pl.multiple_of(s * BW, BW), BW)
        h = [h_all[row, l * TRK : (l + 1) * TRK].astype(f32) for l in range(LOC)]
        for j in range(LOC):
            x = h[0] * k_ref[j : j + 1, :]
            for l in range(1, LOC):
                x = x + h[l] * k_ref[4 * l + j : 4 * l + j + 1, :]
            x_all[row, j * TRK : (j + 1) * TRK] = (-x).astype(bf16)
        return carry

    lax.fori_loop(0, LAYERS, second, 0, unroll=UNROLL2)


def vectors(glob, weight, resid, x_all, q_ref, v_all):
    def term(s, carry):
        wr = (weight[pl.ds(s, 1), :] * resid[pl.ds(s, 1), :]).astype(bf16)
        x = x_all[pl.ds(pl.multiple_of(s * BW, BW), BW), :]
        both = nn(jnp.broadcast_to(wr, (16, PER)), glob[s]) + nt(q_ref[...], x)
        v_all[s // 4, s % 4] = both[:8]
        return carry

    lax.fori_loop(0, LAYERS, term, 0)


def tiles_for(c, start, stop, a0, a1, a2, h_all, x_all):
    right = h_all[pl.ds(pl.multiple_of(c * 2 * BW, 2 * BW), 2 * BW), :]

    def gram(y, carry):
        out = nt(x_all[pl.ds(pl.multiple_of(y * 4 * BW, 4 * BW), 4 * BW), :], right)
        for z in range(4):
            part = out[z * BW : (z + 1) * BW, :]
            a0[y, z, c] = part[0:88, :BW]
            a1[z, c, y, 0:40] = part[88:BW, :BW]
            a1[z, c, y, 40:88] = part[0:48, BW:]
            a2[c, y, z] = part[48:BW, BW:]
        return carry

    lax.fori_loop(start, stop, gram, 0)


def diagonal(c, glob, weight, a0, a1, a2):
    def own(s):
        g = glob[s]
        return nn((jnp.transpose(g.astype(f32)) * weight[pl.ds(s, 1), :]).astype(bf16), g)

    s = 2 * c
    y, z = s // 4, s % 4
    d = own(s)
    a0[y, z, c] += d[0:88]
    a1[z, c, y, 0:40] += d[88:BW]
    d = own(s + 1)
    a1[z + 1, c, y, 40:88] += d[0:48]
    a2[c, y, z + 1] += d[48:BW]


def coords():
    r, c = lax.axis_index("row"), lax.axis_index("col")
    return {"y": r // 4, "z": r % 4, "X": c}


def moved(me, dim, offset, sign):
    if dim == "X":
        x, k = me["X"] // 2, me["X"] % 2
        dx, dk = offset // 2, offset % 2
        return ((x + 4 + sign * dx) % 4) * 2 + (k + dk) % 2
    return (me[dim] + 4 + sign * offset) % 4


def device(me, dim, place):
    at = dict(me)
    at[dim] = place
    return (at["y"] * 4 + at["z"], at["X"])


def offsets(dim):
    return WIDE if dim == "X" else RING


def greet(me, dims):
    barrier = pltpu.get_barrier_semaphore()
    count = 0
    for dim in dims:
        for o in offsets(dim):
            pl.semaphore_signal(
                barrier,
                inc=1,
                device_id=device(me, dim, moved(me, dim, o, 1)),
                device_id_type=MESH,
            )
            count += 1
    return barrier, count


def exchange_kernel(*refs):
    given, refs = refs[:5], refs[5:]
    e, v_out, b, cc = refs[0:3], refs[3], refs[4:7], refs[7:10]
    a = refs[10:13]
    bounce2 = refs[13:16]
    h_all, x_all, v_all, v_mid, sums, q_ref, k_ref = refs[16:23]
    ssem, r1, r2, r3, into_sem, out_sem, v_sem = refs[23:30]
    glob, local, weight, resid, tracks, in_sem = refs[30:36]
    loads = [
        pltpu.make_async_copy(src, dst, in_sem.at[i])
        for i, (src, dst) in enumerate(zip(given, (glob, local, weight, resid, tracks)))
    ]
    for cp in loads:
        cp.start()
    me = coords()
    barrier, count = greet(me, ("y", "z", "X"))
    for cp in loads:
        cp.wait()
    local_terms(glob, local, weight, resid, tracks, h_all, x_all, sums, q_ref, k_ref)
    pl.semaphore_wait(barrier, count)

    def send(src, dst, ssem, rsem, dim, place):
        cp = pltpu.make_async_remote_copy(
            src_ref=src,
            dst_ref=dst,
            send_sem=ssem,
            recv_sem=rsem,
            device_id=device(me, dim, place),
            device_id_type=MESH,
        )
        cp.start()

    def wait_for(ref, sem):
        pltpu.make_async_copy(ref, ref, sem).wait()

    pending = []

    def local_copy(src, mid, dst, sem):
        into = pltpu.make_async_copy(src, mid, into_sem)
        into.start()
        pending.append((into, pltpu.make_async_copy(mid, dst, sem)))

    def flush():
        for into, out in pending:
            into.wait()
            out.start()
        pending.clear()

    def stage1(j):
        o = CHUNKS[j]
        c = moved(me, "X", o, 1)
        for oo in RING:
            to = moved(me, "y", oo, 1)
            send(a[0].at[to, :, c], b[0].at[me["y"], :, c], ssem.at[0, 0], r1.at[0, oo], "y", to)
            to = moved(me, "z", oo, 1)
            send(a[1].at[to, c], b[1].at[me["z"], c], ssem.at[0, 1], r1.at[1, oo], "z", to)
        if o:
            send(a[2].at[c], b[2].at[me["X"]], ssem.at[0, 2], r1.at[2, o], "X", c)

    for j, o in enumerate(CHUNKS):
        c = moved(me, "X", o, 1)
        tiles_for(c, 0, 1, *a, h_all, x_all)
        if j:
            stage1(j - 1)
        tiles_for(c, 1, 4, *a, h_all, x_all)
        diagonal(c, glob, weight, *a)
    vectors(glob, weight, resid, x_all, q_ref, v_all)
    stage1(7)
    for oo in RING:
        to = moved(me, "y", oo, 1)
        send(v_all.at[to], v_mid.at[me["y"]], v_sem.at[0], v_sem.at[1], "y", to)
    v_mid[me["y"]] = v_all[me["y"]]

    for step in range(8):
        for g, order in enumerate(ORDERS):
            d1, d2, _ = order
            offs = (0,) + offsets(d1)
            if step >= len(offs):
                continue
            o1 = offs[step]
            src1 = moved(me, d1, o1, -1)
            if o1:
                wait_for(b[g].at[src1], r1.at[g, o1])
            for o2 in offsets(d2):
                to = moved(me, d2, o2, 1)
                src = b[g].at[src1, to] if o1 else a[g].at[me[d1], to]
                send(src, cc[g].at[me[d2], src1], ssem.at[1, g], r2.at[g, o2], d2, to)
            flush()
            back = cc[g].at[me[d2], src1]
            if o1:
                local_copy(b[g].at[src1, me[d2]], bounce2[g].at[o1], back, out_sem.at[0, g])
            else:
                pltpu.make_async_copy(a[g].at[me[d1], me[d2]], back, out_sem.at[0, g]).start()
    wait_for(v_mid.at[0:3], v_sem.at[1])
    for oo in RING:
        to = moved(me, "z", oo, 1)
        send(v_mid.at[:, to], v_out.at[me["z"]], v_sem.at[2], v_sem.at[3], "z", to)
    v_out[me["z"]] = v_mid[:, me["z"]]
    flush()
    for step in range(8):
        for g, order in enumerate(ORDERS):
            d1, d2, d3 = order
            offs = (0,) + offsets(d2)
            if step >= len(offs):
                continue
            o2 = offs[step]
            src2 = moved(me, d2, o2, -1)
            wait_for(cc[g].at[src2], r2.at[g, o2] if o2 else out_sem.at[0, g])
            for o3 in offsets(d3):
                to = moved(me, d3, o3, 1)
                send(
                    cc[g].at[src2, :, to],
                    e[g].at[me[d3], src2],
                    ssem.at[2, g],
                    r3.at[g],
                    d3,
                    to,
                )
            pltpu.make_async_copy(
                cc[g].at[src2, :, me[d3]], e[g].at[me[d3], src2], out_sem.at[1, g]
            ).start()
    wait_for(v_mid.at[0:3], v_sem.at[3])
    for g, order in enumerate(ORDERS):
        n1, n2, n3 = (SIZE[d] for d in order)
        wait_for(e[g].at[me[order[2]]], out_sem.at[1, g])
        wait_for(e[g].at[0 : n3 - 1], r3.at[g])
        wait_for(b[g].at[0 : n1 - 1], ssem.at[0, g])
        wait_for(cc[g].at[0 : n2 - 1], ssem.at[1, g])
        wait_for(e[g].at[0 : n3 - 1], ssem.at[2, g])
    wait_for(v_mid.at[0:3], v_sem.at[0])
    wait_for(v_mid.at[0:3], v_sem.at[2])


def exchange(glob, local, weight, resid, tracks):
    sizes = [tuple(SIZE[d] for d in order) for order in ORDERS]
    items = [(rows, BW) for rows in ROWS]
    both = list(zip(sizes, items))
    shapes = (
        [pltpu.VMEM((n3, n2, n1) + it, f32) for (n1, n2, n3), it in both]
        + [jax.ShapeDtypeStruct((4, 4, 8, BW), f32)]
        + [jax.ShapeDtypeStruct((n1, n2, n3) + it, f32) for (n1, n2, n3), it in both]
        + [jax.ShapeDtypeStruct((n2, n1, n3) + it, f32) for (n1, n2, n3), it in both]
    )
    any_ = pl.BlockSpec(memory_space=pl.ANY)
    vmem = pl.BlockSpec(memory_space=pltpu.VMEM)
    out = pl.pallas_call(
        exchange_kernel,
        out_shape=tuple(shapes),
        in_specs=[pl.BlockSpec(memory_space=pltpu.HBM)] * 5,
        out_specs=(vmem,) * 3 + (vmem,) + (any_,) * 6,
        scratch_shapes=[pltpu.VMEM(n + it, f32) for n, it in both]
        + [pltpu.VMEM((n1, n3) + it, f32) for (n1, n2, n3), it in both]
        + [
            pltpu.VMEM((LAYERS * BW, LOC * TRK), bf16),
            pltpu.VMEM((LAYERS * BW, LOC * TRK), bf16),
            pltpu.VMEM((4, 4, 8, BW), f32),
            pltpu.VMEM((4, 4, 8, BW), f32),
            pltpu.VMEM((24, TRK), f32),
            pltpu.VMEM((16, LOC * TRK), bf16),
            pltpu.VMEM((16, TRK), f32),
            pltpu.SemaphoreType.DMA((3, 3)),
            pltpu.SemaphoreType.DMA((3, 8)),
            pltpu.SemaphoreType.DMA((3, 8)),
            pltpu.SemaphoreType.DMA((3,)),
            pltpu.SemaphoreType.DMA,
            pltpu.SemaphoreType.DMA((2, 3)),
            pltpu.SemaphoreType.DMA((4,)),
            pltpu.VMEM(glob.shape, bf16),
            pltpu.VMEM(local.shape, f32),
            pltpu.VMEM(weight.shape, f32),
            pltpu.VMEM(resid.shape, f32),
            pltpu.VMEM(tracks.shape, jnp.int32),
            pltpu.SemaphoreType.DMA((5,)),
        ],
        compiler_params=pltpu.CompilerParams(
            collective_id=0, has_side_effects=True, vmem_limit_bytes=36 << 20
        ),
        name="exchange",
    )(glob, local, weight, resid, tracks)
    return out[:4]


def place_kernel(
    given_b, given_w, e0, e1, e2, vec, schur, product, diag, acc0, acc1, w_ref, p_ref, blocks, weak, rhs, sem, lsem
):
    row, col = lax.axis_index("row"), lax.axis_index("col")

    load_b = pltpu.make_async_copy(given_b, blocks, lsem.at[0])
    load_w = pltpu.make_async_copy(given_w, weak, lsem.at[1])
    load_b.start()
    load_w.start()
    acc0[...] = jnp.zeros_like(acc0)
    acc1[...] = jnp.zeros_like(acc1)
    rhs[...] = jnp.zeros_like(rhs)
    load_w.wait()
    load_b.wait()
    w = weak[...]
    w_hi = w.astype(bf16)
    w_ref[0:64, :] = w_hi
    w_ref[64:128, :] = (w - w_hi.astype(f32)).astype(bf16)
    p_ref[...] = jnp.zeros_like(p_ref)

    def term(i, carry):
        k = blocks[row, i * 8 + col]
        rhs[pl.ds(k, 1), :] += vec[i % 4, i // 4, 0:1]
        return carry

    lax.fori_loop(0, 16, term, 0)

    def batch(xb, carry):
        def bundle(i, carry):
            y, z = i // 4, i % 4
            b = i * 8 + xb
            l0 = pl.ds(pl.multiple_of(blocks[2 * col, b] * BW, BW), BW)
            l1 = pl.ds(pl.multiple_of(blocks[2 * col + 1, b] * BW, BW), BW)
            r = pl.multiple_of(blocks[row, b] * BW, BW)
            top, low = pl.ds(r, 88), pl.ds(r + 88, 40)
            head, rest = pl.ds(r, 48), pl.ds(r + 48, 80)
            v_top = acc0[top, l0] + e0[xb, z, y]
            v_head = acc1[head, l1] + e1[y, xb, z, 40:88]
            v_low = acc0[low, l0] + e1[y, xb, z, 0:40]
            v_rest = acc1[rest, l1] + e2[z, y, xb]
            acc0[top, l0] = v_top
            acc1[head, l1] = v_head
            acc0[low, l0] = v_low
            acc1[rest, l1] = v_rest
            return carry

        return lax.fori_loop(0, 16, bundle, carry, unroll=4)

    lax.fori_loop(0, 8, batch, 0)

    def finish_half(half, acc):
        def copy_out(ch):
            cols = pl.ds(pl.multiple_of(ch * 256, 256), 256)
            there = pl.ds(pl.multiple_of(half * GB * BW + ch * 256, 256), 256)
            return pltpu.make_async_copy(
                acc.at[:, cols], schur.at[:, there], sem.at[half * 4 + ch]
            )

        def chunk(ch, carry):
            cols = pl.ds(pl.multiple_of(ch * 256, 256), 256)
            wc = w_ref[:, pl.ds(pl.multiple_of(half * GB * BW + ch * 256, 256), 256)]
            v = acc[:, cols]
            hi = v.astype(bf16)
            lo = (v - hi.astype(f32)).astype(bf16)
            p_ref[...] += nt(hi, wc) + nt(lo, wc)

            @pl.when(row % 2 == half)
            def _():
                for m in range(2):
                    k = 2 * ch + m
                    at = pl.ds(pl.multiple_of(k * BW, BW), BW)
                    diag[k // 2, m] = acc[at, at]

                @pl.when(col == row // 2)
                def _():
                    acc[:, cols] = jnp.zeros((GB * BW, 256), f32)

            copy_out(ch).start()
            return carry

        lax.fori_loop(0, 4, chunk, 0)
        return copy_out

    outs = [finish_half(0, acc0), finish_half(1, acc1)]
    for k in range(GB):
        pt = jnp.transpose(p_ref[k * BW : (k + 1) * BW, :])
        product[k // 2, k % 2, 0:64] = pt[0:64] + pt[64:128]
        product[k // 2, k % 2, 64:72] = rhs[...]
    for copy_out in outs:
        for ch in range(4):
            copy_out(ch).wait()


def place(blocks, weak, e0, e1, e2, vec):
    vmem = pl.BlockSpec(memory_space=pltpu.VMEM)
    any_ = pl.BlockSpec(memory_space=pl.ANY)
    hbm = pl.BlockSpec(memory_space=pltpu.HBM)
    return pl.pallas_call(
        place_kernel,
        in_specs=[hbm, hbm, vmem, vmem, vmem, vmem],
        out_specs=(any_, vmem, vmem),
        out_shape=(
            jax.ShapeDtypeStruct((GB * BW, 2 * GB * BW), f32),
            jax.ShapeDtypeStruct((4, 2, 72, BW), f32),
            jax.ShapeDtypeStruct((4, 2, BW, BW), f32),
        ),
        scratch_shapes=[
            pltpu.VMEM((GB * BW, GB * BW), f32),
            pltpu.VMEM((GB * BW, GB * BW), f32),
            pltpu.VMEM((BW, 2 * GB * BW), bf16),
            pltpu.VMEM((GB * BW, BW), f32),
            pltpu.SMEM(blocks.shape, jnp.int32),
            pltpu.VMEM(weak.shape, f32),
            pltpu.VMEM((GB, BW), f32),
            pltpu.SemaphoreType.DMA((8,)),
            pltpu.SemaphoreType.DMA((2,)),
        ],
        compiler_params=pltpu.CompilerParams(vmem_limit_bytes=20 << 20),
        name="place",
    )(blocks, weak, e0, e1, e2, vec)


def finish_kernel(product, diag, weak, tile, rhs, near, chip, far, spare, ssem, rsem):
    me = coords()
    row = lax.axis_index("row")
    mine = me["X"]
    x, k = mine // 2, mine % 2
    owner = row // 2
    barrier, count = greet(me, ("X",))
    pl.semaphore_wait(barrier, count)

    def copy(src, dst, i, to):
        return pltpu.make_async_remote_copy(
            src_ref=src,
            dst_ref=dst,
            send_sem=ssem.at[i],
            recv_sem=rsem.at[i],
            device_id=device(me, "X", to),
            device_id_type=MESH,
        )

    def wait_for(ref, sem):
        pltpu.make_async_copy(ref, ref, sem).wait()

    copy(product.at[:, 1 - k], near, 0, moved(me, "X", 1, 1)).start()

    @pl.when(mine == owner)
    def _():
        for o in WIDE:
            to = moved(me, "X", o, 1)
            copy(diag.at[to // 2, to % 2], tile, 2, to).start()
        tile[...] = diag[x, k]

    wait_for(near, rsem.at[0])
    for i in range(4):
        chip[i] = product[i, k] + near[i]
    wait_for(near, ssem.at[0])
    for dx in (2, 1, 3):
        to = moved(me, "X", 2 * dx, 1)
        copy(chip.at[to // 2], far.at[dx - 1], 1, to).start()
    total = chip[x]
    wait_for(far, rsem.at[1])
    total = total + far[0] + far[1] + far[2]
    weak[...] = total[0:64]
    rhs[...] = total[64:72]
    wait_for(far, ssem.at[1])

    @pl.when(mine != owner)
    def _():
        wait_for(tile, rsem.at[2])

    @pl.when(mine == owner)
    def _():
        wait_for(spare, ssem.at[2])


def finish(product, diag):
    vmem = pl.BlockSpec(memory_space=pltpu.VMEM)
    return pl.pallas_call(
        finish_kernel,
        out_shape=(
            jax.ShapeDtypeStruct((64, BW), f32),
            jax.ShapeDtypeStruct((BW, BW), f32),
            jax.ShapeDtypeStruct((GB, BW), f32),
        ),
        in_specs=[vmem] * 2,
        out_specs=(vmem,) * 3,
        scratch_shapes=[
            pltpu.VMEM((4, 72, BW), f32),
            pltpu.VMEM((4, 72, BW), f32),
            pltpu.VMEM((3, 72, BW), f32),
            pltpu.VMEM((7, BW, BW), f32),
            pltpu.SemaphoreType.DMA((3,)),
            pltpu.SemaphoreType.DMA((3,)),
        ],
        compiler_params=pltpu.CompilerParams(
            collective_id=1, has_side_effects=True, vmem_limit_bytes=8 << 20
        ),
        name="finish",
    )(product, diag)


def emit_kernel(weak_in, tile, rhs_in, weak, layer, rhs):
    col = lax.axis_index("col")
    weak[...] = weak_in[...]
    rhs[...] = rhs_in[...]
    layer[...] = jnp.zeros_like(layer)
    layer[pl.ds(pl.multiple_of(col * BW, BW), BW), :] = tile[...]


def emit(weak, tile, rhs):
    vmem = pl.BlockSpec(memory_space=pltpu.VMEM)
    return pl.pallas_call(
        emit_kernel,
        out_shape=(
            jax.ShapeDtypeStruct((64, BW), f32),
            jax.ShapeDtypeStruct((GB * BW, BW), f32),
            jax.ShapeDtypeStruct((GB, BW), f32),
        ),
        in_specs=[vmem] * 3,
        out_specs=(vmem,) * 3,
        compiler_params=pltpu.CompilerParams(vmem_limit_bytes=8 << 20),
        name="emit",
    )(weak, tile, rhs)


def body(glob_derivs, local_derivs, weights, residuals, track_ids, module_blocks, weak_modes):
    def stay(v):
        return pltpu.with_memory_space_constraint(v, pltpu.HBM)

    inputs = (glob_derivs, local_derivs, weights, residuals, track_ids)
    e = exchange(*[stay(v[0]) for v in inputs])
    schur, product, diag = place(stay(module_blocks.T), stay(weak_modes.T), *e)
    weak, layer, rhs = emit(*finish(product, diag))
    return schur, layer, rhs.reshape(GB * BW), weak.T


def solution(mesh):
    placed = (
        P(("row", "col"), None, None, None),
        P(("row", "col"), None, None, None),
        P(("row", "col"), None, None),
        P(("row", "col"), None, None),
        P(("row", "col"), None, None),
        P(),
        P("col", None),
    )
    return jax.shard_map(
        body,
        mesh=mesh,
        in_specs=placed,
        out_specs=(P("row", "col"), P("row", "col"), P("row"), P(("row", "col"), None)),
        check_vma=False,
    )
```

```python
import functools

import jax
import jax.numpy as jnp
from jax import lax
from jax.experimental import pallas as pl
from jax.experimental.pallas import tpu as pltpu
from jax.sharding import PartitionSpec as P

BW = 128
GB = 8
LOC = 4
TRK = 256
LAYERS = 16
PER = 256
ROWS = (88, 88, 80)
SIZE = {"y": 4, "z": 4, "X": 8}
ORDERS = (("y", "z", "X"), ("z", "X", "y"), ("X", "y", "z"))
RING = (1, 3, 2)
WIDE = (2, 6, 3, 7, 4, 5, 1)
UNROLL1 = 4
UNROLL2 = 4
CHUNKS = (2, 6, 3, 7, 0, 4, 5, 1)
MESH = pl.DeviceIdType.MESH
f32 = jnp.float32
bf16 = jnp.bfloat16


def split3(v):
    hi = v.astype(bf16)
    rest = v - hi.astype(f32)
    mid = rest.astype(bf16)
    low = (rest - mid.astype(f32)).astype(bf16)
    return hi, mid, low


def nt(a, b):
    return lax.dot_general(a, b, (((1,), (1,)), ((), ())), preferred_element_type=f32)


def nn(a, b):
    return lax.dot_general(a, b, (((1,), (0,)), ((), ())), preferred_element_type=f32)


def local_terms(glob, local, weight, resid, tracks, h_all, x_all, sums, q_ref, k_ref):
    sums[...] = jnp.zeros_like(sums)

    def first(s, carry):
        gt_low = jnp.transpose(glob[s].astype(f32)).astype(bf16)
        t = tracks[pl.ds(s, 1), :]
        w = weight[pl.ds(s, 1), :]
        r = resid[pl.ds(s, 1), :]
        hot = lax.broadcasted_iota(jnp.int32, (TRK, PER), 0) == t
        a = local[s]
        wa = w * a
        zero = jnp.zeros((), f32)
        row = pl.ds(pl.multiple_of(s * BW, BW), BW)
        for j in range(LOC):
            spread = jnp.where(hot, wa[j : j + 1, :], zero).astype(bf16)
            h_all[row, j * TRK : (j + 1) * TRK] = nt(gt_low, spread).astype(bf16)
        terms = []
        for i in range(LOC):
            terms.append(wa[i : i + 1, :] * a)
        terms.append(wa * r)
        terms.append(jnp.zeros((12, PER), f32))
        stacked = jnp.concatenate(terms, axis=0)
        hot_low = jnp.where(hot, jnp.ones((), f32), zero).astype(bf16)
        sums[...] += nt(jnp.concatenate(split3(stacked), axis=0), hot_low)
        return carry

    lax.fori_loop(0, LAYERS, first, 0, unroll=UNROLL1)

    total = sums[0:32] + sums[32:64] + sums[64:96]
    one = jnp.ones((1, TRK), f32)
    nil = jnp.zeros((1, TRK), f32)
    rows = [
        [total[4 * i + j : 4 * i + j + 1, :] + (one if i == j else nil) for j in range(LOC)]
        for i in range(LOC)
    ]
    inv = [[one if i == j else nil for j in range(LOC)] for i in range(LOC)]
    for p in range(LOC):
        pivot = rows[p][p]
        scaled = [v / pivot for v in rows[p]]
        scaled_inv = [v / pivot for v in inv[p]]
        for o in range(LOC):
            if o != p:
                factor = rows[o][p]
                rows[o] = [u - factor * v for u, v in zip(rows[o], scaled)]
                inv[o] = [u - factor * v for u, v in zip(inv[o], scaled_inv)]
        rows[p] = scaled
        inv[p] = scaled_inv
    for i in range(LOC):
        for j in range(LOC):
            k_ref[4 * i + j : 4 * i + j + 1, :] = -inv[i][j]
    for j in range(LOC):
        q_ref[:, j * TRK : (j + 1) * TRK] = jnp.broadcast_to(
            total[16 + j : 17 + j, :].astype(bf16), (16, TRK)
        )

    def second(s, carry):
        row = pl.ds(pl.multiple_of(s * BW, BW), BW)
        h = [h_all[row, l * TRK : (l + 1) * TRK].astype(f32) for l in range(LOC)]
        for j in range(LOC):
            x = h[0] * k_ref[j : j + 1, :]
            for l in range(1, LOC):
                x = x + h[l] * k_ref[4 * l + j : 4 * l + j + 1, :]
            x_all[row, j * TRK : (j + 1) * TRK] = x.astype(bf16)
        return carry

    lax.fori_loop(0, LAYERS, second, 0, unroll=UNROLL2)


def vectors(glob, weight, resid, x_all, q_ref, v_all):
    def term(s, carry):
        wr = (weight[pl.ds(s, 1), :] * resid[pl.ds(s, 1), :]).astype(bf16)
        x = x_all[pl.ds(pl.multiple_of(s * BW, BW), BW), :]
        both = nn(jnp.broadcast_to(wr, (16, PER)), glob[s]) + nt(q_ref[...], x)
        v_all[s // 4, s % 4] = both[:8]
        return carry

    lax.fori_loop(0, LAYERS, term, 0)


def tiles_for(c, start, stop, a0, a1, a2, h_all, x_all):
    right = h_all[pl.ds(pl.multiple_of(c * 2 * BW, 2 * BW), 2 * BW), :]

    def gram(y, carry):
        out = nt(x_all[pl.ds(pl.multiple_of(y * 4 * BW, 4 * BW), 4 * BW), :], right)
        for z in range(4):
            part = out[z * BW : (z + 1) * BW, :]
            a0[y, z, c] = part[0:88, :BW]
            a1[z, c, y, 0:40] = part[88:BW, :BW]
            a1[z, c, y, 40:88] = part[0:48, BW:]
            a2[c, y, z] = part[48:BW, BW:]
        return carry

    lax.fori_loop(start, stop, gram, 0)


def diagonal(c, glob, weight, a0, a1, a2):
    def own(s):
        g = glob[s]
        return nn((jnp.transpose(g.astype(f32)) * weight[pl.ds(s, 1), :]).astype(bf16), g)

    s = 2 * c
    y, z = s // 4, s % 4
    d = own(s)
    a0[y, z, c] += d[0:88]
    a1[z, c, y, 0:40] += d[88:BW]
    d = own(s + 1)
    a1[z + 1, c, y, 40:88] += d[0:48]
    a2[c, y, z + 1] += d[48:BW]


def coords():
    r, c = lax.axis_index("row"), lax.axis_index("col")
    return {"y": r // 4, "z": r % 4, "X": c}


def moved(me, dim, offset, sign):
    if dim == "X":
        x, k = me["X"] // 2, me["X"] % 2
        dx, dk = offset // 2, offset % 2
        return ((x + 4 + sign * dx) % 4) * 2 + (k + dk) % 2
    return (me[dim] + 4 + sign * offset) % 4


def device(me, dim, place):
    at = dict(me)
    at[dim] = place
    return (at["y"] * 4 + at["z"], at["X"])


def offsets(dim):
    return WIDE if dim == "X" else RING


def greet(me, dims):
    barrier = pltpu.get_barrier_semaphore()
    count = 0
    for dim in dims:
        for o in offsets(dim):
            pl.semaphore_signal(
                barrier,
                inc=1,
                device_id=device(me, dim, moved(me, dim, o, 1)),
                device_id_type=MESH,
            )
            count += 1
    return barrier, count


def exchange_kernel(*refs):
    given, refs = refs[:5], refs[5:]
    e, v_out, b, cc = refs[0:3], refs[3], refs[4:7], refs[7:10]
    a = refs[10:13]
    bounce2 = refs[13:16]
    h_all, x_all, v_all, v_mid, sums, q_ref, k_ref = refs[16:23]
    ssem, r1, r2, r3, into_sem, out_sem, v_sem = refs[23:30]
    glob, local, weight, resid, tracks, in_sem = refs[30:36]
    loads = [
        pltpu.make_async_copy(src, dst, in_sem.at[i])
        for i, (src, dst) in enumerate(zip(given, (glob, local, weight, resid, tracks)))
    ]
    for cp in loads:
        cp.start()
    me = coords()
    barrier, count = greet(me, ("y", "z", "X"))
    for cp in loads:
        cp.wait()
    local_terms(glob, local, weight, resid, tracks, h_all, x_all, sums, q_ref, k_ref)
    pl.semaphore_wait(barrier, count)

    def send(src, dst, ssem, rsem, dim, place):
        cp = pltpu.make_async_remote_copy(
            src_ref=src,
            dst_ref=dst,
            send_sem=ssem,
            recv_sem=rsem,
            device_id=device(me, dim, place),
            device_id_type=MESH,
        )
        cp.start()

    def wait_for(ref, sem):
        pltpu.make_async_copy(ref, ref, sem).wait()

    pending = []

    def local_copy(src, mid, dst, sem):
        into = pltpu.make_async_copy(src, mid, into_sem)
        into.start()
        pending.append((into, pltpu.make_async_copy(mid, dst, sem)))

    def flush():
        for into, out in pending:
            into.wait()
            out.start()
        pending.clear()

    def stage1(j):
        o = CHUNKS[j]
        c = moved(me, "X", o, 1)
        for oo in RING:
            to = moved(me, "y", oo, 1)
            send(a[0].at[to, :, c], b[0].at[me["y"], :, c], ssem.at[0, 0], r1.at[0, oo], "y", to)
            to = moved(me, "z", oo, 1)
            send(a[1].at[to, c], b[1].at[me["z"], c], ssem.at[0, 1], r1.at[1, oo], "z", to)
        if o:
            send(a[2].at[c], b[2].at[me["X"]], ssem.at[0, 2], r1.at[2, o], "X", c)

    for j, o in enumerate(CHUNKS):
        c = moved(me, "X", o, 1)
        tiles_for(c, 0, 1, *a, h_all, x_all)
        if j:
            stage1(j - 1)
        tiles_for(c, 1, 4, *a, h_all, x_all)
        diagonal(c, glob, weight, *a)
    vectors(glob, weight, resid, x_all, q_ref, v_all)
    stage1(7)
    for oo in RING:
        to = moved(me, "y", oo, 1)
        send(v_all.at[to], v_mid.at[me["y"]], v_sem.at[0], v_sem.at[1], "y", to)
    v_mid[me["y"]] = v_all[me["y"]]

    for step in range(8):
        for g, order in enumerate(ORDERS):
            d1, d2, _ = order
            offs = (0,) + offsets(d1)
            if step >= len(offs):
                continue
            o1 = offs[step]
            src1 = moved(me, d1, o1, -1)
            if o1:
                wait_for(b[g].at[src1], r1.at[g, o1])
            for o2 in offsets(d2):
                to = moved(me, d2, o2, 1)
                src = b[g].at[src1, to] if o1 else a[g].at[me[d1], to]
                send(src, cc[g].at[me[d2], src1], ssem.at[1, g], r2.at[g, o2], d2, to)
            flush()
            back = cc[g].at[me[d2], src1]
            if o1:
                local_copy(b[g].at[src1, me[d2]], bounce2[g].at[o1], back, out_sem.at[0, g])
            else:
                pltpu.make_async_copy(a[g].at[me[d1], me[d2]], back, out_sem.at[0, g]).start()
    wait_for(v_mid.at[0:3], v_sem.at[1])
    for oo in RING:
        to = moved(me, "z", oo, 1)
        send(v_mid.at[:, to], v_out.at[me["z"]], v_sem.at[2], v_sem.at[3], "z", to)
    v_out[me["z"]] = v_mid[:, me["z"]]
    flush()
    for step in range(8):
        for g, order in enumerate(ORDERS):
            d1, d2, d3 = order
            offs = (0,) + offsets(d2)
            if step >= len(offs):
                continue
            o2 = offs[step]
            src2 = moved(me, d2, o2, -1)
            wait_for(cc[g].at[src2], r2.at[g, o2] if o2 else out_sem.at[0, g])
            for o3 in offsets(d3):
                to = moved(me, d3, o3, 1)
                send(
                    cc[g].at[src2, :, to],
                    e[g].at[me[d3], src2],
                    ssem.at[2, g],
                    r3.at[g],
                    d3,
                    to,
                )
            pltpu.make_async_copy(
                cc[g].at[src2, :, me[d3]], e[g].at[me[d3], src2], out_sem.at[1, g]
            ).start()
    wait_for(v_mid.at[0:3], v_sem.at[3])
    for g, order in enumerate(ORDERS):
        n1, n2, n3 = (SIZE[d] for d in order)
        wait_for(e[g].at[me[order[2]]], out_sem.at[1, g])
        wait_for(e[g].at[0 : n3 - 1], r3.at[g])
        wait_for(b[g].at[0 : n1 - 1], ssem.at[0, g])
        wait_for(cc[g].at[0 : n2 - 1], ssem.at[1, g])
        wait_for(e[g].at[0 : n3 - 1], ssem.at[2, g])
    wait_for(v_mid.at[0:3], v_sem.at[0])
    wait_for(v_mid.at[0:3], v_sem.at[2])


def exchange(glob, local, weight, resid, tracks):
    sizes = [tuple(SIZE[d] for d in order) for order in ORDERS]
    items = [(rows, BW) for rows in ROWS]
    both = list(zip(sizes, items))
    shapes = (
        [pltpu.VMEM((n3, n2, n1) + it, f32) for (n1, n2, n3), it in both]
        + [jax.ShapeDtypeStruct((4, 4, 8, BW), f32)]
        + [jax.ShapeDtypeStruct((n1, n2, n3) + it, f32) for (n1, n2, n3), it in both]
        + [jax.ShapeDtypeStruct((n2, n1, n3) + it, f32) for (n1, n2, n3), it in both]
    )
    any_ = pl.BlockSpec(memory_space=pl.ANY)
    vmem = pl.BlockSpec(memory_space=pltpu.VMEM)
    out = pl.pallas_call(
        exchange_kernel,
        out_shape=tuple(shapes),
        in_specs=[pl.BlockSpec(memory_space=pltpu.HBM)] * 5,
        out_specs=(vmem,) * 3 + (vmem,) + (any_,) * 6,
        scratch_shapes=[pltpu.VMEM(n + it, f32) for n, it in both]
        + [pltpu.VMEM((n1, n3) + it, f32) for (n1, n2, n3), it in both]
        + [
            pltpu.VMEM((LAYERS * BW, LOC * TRK), bf16),
            pltpu.VMEM((LAYERS * BW, LOC * TRK), bf16),
            pltpu.VMEM((4, 4, 8, BW), f32),
            pltpu.VMEM((4, 4, 8, BW), f32),
            pltpu.VMEM((96, TRK), f32),
            pltpu.VMEM((16, LOC * TRK), bf16),
            pltpu.VMEM((16, TRK), f32),
            pltpu.SemaphoreType.DMA((3, 3)),
            pltpu.SemaphoreType.DMA((3, 8)),
            pltpu.SemaphoreType.DMA((3, 8)),
            pltpu.SemaphoreType.DMA((3,)),
            pltpu.SemaphoreType.DMA,
            pltpu.SemaphoreType.DMA((2, 3)),
            pltpu.SemaphoreType.DMA((4,)),
            pltpu.VMEM(glob.shape, bf16),
            pltpu.VMEM(local.shape, f32),
            pltpu.VMEM(weight.shape, f32),
            pltpu.VMEM(resid.shape, f32),
            pltpu.VMEM(tracks.shape, jnp.int32),
            pltpu.SemaphoreType.DMA((5,)),
        ],
        compiler_params=pltpu.CompilerParams(
            collective_id=0, has_side_effects=True, vmem_limit_bytes=36 << 20
        ),
        name="exchange",
    )(glob, local, weight, resid, tracks)
    return out[:4]


def place_kernel(
    given_b, given_w, e0, e1, e2, vec, schur, product, diag, acc0, acc1, w_ref, p_ref, blocks, weak, rhs, sem, lsem
):
    row, col = lax.axis_index("row"), lax.axis_index("col")

    load_b = pltpu.make_async_copy(given_b, blocks, lsem.at[0])
    load_w = pltpu.make_async_copy(given_w, weak, lsem.at[1])
    load_b.start()
    load_w.start()
    acc0[...] = jnp.zeros_like(acc0)
    acc1[...] = jnp.zeros_like(acc1)
    rhs[...] = jnp.zeros_like(rhs)
    load_b.wait()

    def term(i, carry):
        k = blocks[row, i * 8 + col]
        rhs[pl.ds(k, 1), :] += vec[i % 4, i // 4, 0:1]
        return carry

    lax.fori_loop(0, 16, term, 0)

    def batch(xb, carry):
        def bundle(i, carry):
            y, z = i // 4, i % 4
            b = i * 8 + xb
            l0 = pl.ds(pl.multiple_of(blocks[2 * col, b] * BW, BW), BW)
            l1 = pl.ds(pl.multiple_of(blocks[2 * col + 1, b] * BW, BW), BW)
            r = pl.multiple_of(blocks[row, b] * BW, BW)
            top, low = pl.ds(r, 88), pl.ds(r + 88, 40)
            head, rest = pl.ds(r, 48), pl.ds(r + 48, 80)
            v_top = acc0[top, l0] + e0[xb, z, y]
            v_head = acc1[head, l1] + e1[y, xb, z, 40:88]
            v_low = acc0[low, l0] + e1[y, xb, z, 0:40]
            v_rest = acc1[rest, l1] + e2[z, y, xb]
            acc0[top, l0] = v_top
            acc1[head, l1] = v_head
            acc0[low, l0] = v_low
            acc1[rest, l1] = v_rest
            return carry

        return lax.fori_loop(0, 16, bundle, carry, unroll=4)

    lax.fori_loop(0, 8, batch, 0)
    load_w.wait()
    w = weak[...]
    w_hi = w.astype(bf16)
    w_ref[0:64, :] = w_hi
    w_ref[64:128, :] = (w - w_hi.astype(f32)).astype(bf16)
    p_ref[...] = jnp.zeros_like(p_ref)


    def finish_half(half, acc):
        def copy_out(ch):
            cols = pl.ds(pl.multiple_of(ch * 256, 256), 256)
            there = pl.ds(pl.multiple_of(half * GB * BW + ch * 256, 256), 256)
            return pltpu.make_async_copy(
                acc.at[:, cols], schur.at[:, there], sem.at[half * 4 + ch]
            )

        def chunk(ch, carry):
            cols = pl.ds(pl.multiple_of(ch * 256, 256), 256)
            wc = w_ref[:, pl.ds(pl.multiple_of(half * GB * BW + ch * 256, 256), 256)]
            v = acc[:, cols]
            hi = v.astype(bf16)
            lo = (v - hi.astype(f32)).astype(bf16)
            p_ref[...] += nt(hi, wc) + nt(lo, wc)

            @pl.when(row % 2 == half)
            def _():
                for m in range(2):
                    k = 2 * ch + m
                    at = pl.ds(pl.multiple_of(k * BW, BW), BW)
                    diag[k // 2, m] = acc[at, at]

                @pl.when(col == row // 2)
                def _():
                    acc[:, cols] = jnp.zeros((GB * BW, 256), f32)

            copy_out(ch).start()
            return carry

        lax.fori_loop(0, 4, chunk, 0)
        return copy_out

    outs = [finish_half(0, acc0), finish_half(1, acc1)]
    for k in range(GB):
        pt = jnp.transpose(p_ref[k * BW : (k + 1) * BW, :])
        product[k // 2, k % 2, 0:64] = pt[0:64] + pt[64:128]
        product[k // 2, k % 2, 64:72] = rhs[...]
    for copy_out in outs:
        for ch in range(4):
            copy_out(ch).wait()


def place(blocks, weak, e0, e1, e2, vec):
    vmem = pl.BlockSpec(memory_space=pltpu.VMEM)
    any_ = pl.BlockSpec(memory_space=pl.ANY)
    hbm = pl.BlockSpec(memory_space=pltpu.HBM)
    return pl.pallas_call(
        place_kernel,
        in_specs=[hbm, hbm, vmem, vmem, vmem, vmem],
        out_specs=(any_, vmem, vmem),
        out_shape=(
            jax.ShapeDtypeStruct((GB * BW, 2 * GB * BW), f32),
            jax.ShapeDtypeStruct((4, 2, 72, BW), f32),
            jax.ShapeDtypeStruct((4, 2, BW, BW), f32),
        ),
        scratch_shapes=[
            pltpu.VMEM((GB * BW, GB * BW), f32),
            pltpu.VMEM((GB * BW, GB * BW), f32),
            pltpu.VMEM((BW, 2 * GB * BW), bf16),
            pltpu.VMEM((GB * BW, BW), f32),
            pltpu.SMEM(blocks.shape, jnp.int32),
            pltpu.VMEM(weak.shape, f32),
            pltpu.VMEM((GB, BW), f32),
            pltpu.SemaphoreType.DMA((8,)),
            pltpu.SemaphoreType.DMA((2,)),
        ],
        compiler_params=pltpu.CompilerParams(vmem_limit_bytes=20 << 20),
        name="place",
    )(blocks, weak, e0, e1, e2, vec)


def finish_kernel(product, diag, weak, tile, rhs, near, chip, far, spare, ssem, rsem):
    me = coords()
    row = lax.axis_index("row")
    mine = me["X"]
    x, k = mine // 2, mine % 2
    owner = row // 2
    barrier, count = greet(me, ("X",))
    pl.semaphore_wait(barrier, count)

    def copy(src, dst, i, to):
        return pltpu.make_async_remote_copy(
            src_ref=src,
            dst_ref=dst,
            send_sem=ssem.at[i],
            recv_sem=rsem.at[i],
            device_id=device(me, "X", to),
            device_id_type=MESH,
        )

    def wait_for(ref, sem):
        pltpu.make_async_copy(ref, ref, sem).wait()

    copy(product.at[:, 1 - k], near, 0, moved(me, "X", 1, 1)).start()

    @pl.when(mine == owner)
    def _():
        for o in WIDE:
            to = moved(me, "X", o, 1)
            copy(diag.at[to // 2, to % 2], tile, 2, to).start()
        tile[...] = diag[x, k]

    wait_for(near, rsem.at[0])
    for i in range(4):
        chip[i] = product[i, k] + near[i]
    wait_for(near, ssem.at[0])
    for dx in (2, 1, 3):
        to = moved(me, "X", 2 * dx, 1)
        copy(chip.at[to // 2], far.at[dx - 1], 1, to).start()
    total = chip[x]
    wait_for(far, rsem.at[1])
    total = total + far[0] + far[1] + far[2]
    weak[...] = total[0:64]
    rhs[...] = total[64:72]
    wait_for(far, ssem.at[1])

    @pl.when(mine != owner)
    def _():
        wait_for(tile, rsem.at[2])

    @pl.when(mine == owner)
    def _():
        wait_for(spare, ssem.at[2])


def finish(product, diag):
    vmem = pl.BlockSpec(memory_space=pltpu.VMEM)
    return pl.pallas_call(
        finish_kernel,
        out_shape=(
            jax.ShapeDtypeStruct((64, BW), f32),
            jax.ShapeDtypeStruct((BW, BW), f32),
            jax.ShapeDtypeStruct((GB, BW), f32),
        ),
        in_specs=[vmem] * 2,
        out_specs=(vmem,) * 3,
        scratch_shapes=[
            pltpu.VMEM((4, 72, BW), f32),
            pltpu.VMEM((4, 72, BW), f32),
            pltpu.VMEM((3, 72, BW), f32),
            pltpu.VMEM((7, BW, BW), f32),
            pltpu.SemaphoreType.DMA((3,)),
            pltpu.SemaphoreType.DMA((3,)),
        ],
        compiler_params=pltpu.CompilerParams(
            collective_id=1, has_side_effects=True, vmem_limit_bytes=8 << 20
        ),
        name="finish",
    )(product, diag)


def emit_kernel(weak_in, tile, rhs_in, weak, layer, rhs):
    col = lax.axis_index("col")
    weak[...] = weak_in[...]
    rhs[...] = rhs_in[...]
    layer[...] = jnp.zeros_like(layer)
    layer[pl.ds(pl.multiple_of(col * BW, BW), BW), :] = tile[...]


def emit(weak, tile, rhs):
    vmem = pl.BlockSpec(memory_space=pltpu.VMEM)
    return pl.pallas_call(
        emit_kernel,
        out_shape=(
            jax.ShapeDtypeStruct((64, BW), f32),
            jax.ShapeDtypeStruct((GB * BW, BW), f32),
            jax.ShapeDtypeStruct((GB, BW), f32),
        ),
        in_specs=[vmem] * 3,
        out_specs=(vmem,) * 3,
        compiler_params=pltpu.CompilerParams(vmem_limit_bytes=8 << 20),
        name="emit",
    )(weak, tile, rhs)


def body(glob_derivs, local_derivs, weights, residuals, track_ids, module_blocks, weak_modes):
    def stay(v):
        return pltpu.with_memory_space_constraint(v, pltpu.HBM)

    inputs = (glob_derivs, local_derivs, weights, residuals, track_ids)
    e = exchange(*[stay(v[0]) for v in inputs])
    schur, product, diag = place(stay(module_blocks.T), stay(weak_modes.T), *e)
    weak, layer, rhs = emit(*finish(product, diag))
    return schur, layer, rhs.reshape(GB * BW), weak.T


def solution(mesh):
    placed = (
        P(("row", "col"), None, None, None),
        P(("row", "col"), None, None, None),
        P(("row", "col"), None, None),
        P(("row", "col"), None, None),
        P(("row", "col"), None, None),
        P(),
        P("col", None),
    )
    return jax.shard_map(
        body,
        mesh=mesh,
        in_specs=placed,
        out_specs=(P("row", "col"), P("row", "col"), P("row"), P(("row", "col"), None)),
        check_vma=False,
    )
```

```python
import functools

import jax
import jax.numpy as jnp
from jax import lax
from jax.experimental import pallas as pl
from jax.experimental.pallas import tpu as pltpu
from jax.sharding import PartitionSpec as P

BW = 128
GB = 8
LOC = 4
TRK = 256
LAYERS = 16
PER = 256
ROWS = (88, 88, 80)
SIZE = {"y": 4, "z": 4, "X": 8}
ORDERS = (("y", "z", "X"), ("z", "X", "y"), ("X", "y", "z"))
RING = (1, 3, 2)
WIDE = (2, 6, 3, 7, 4, 5, 1)
UNROLL1 = 4
UNROLL2 = 4
CHUNKS = (2, 6, 3, 7, 0, 4, 5, 1)
MESH = pl.DeviceIdType.MESH
f32 = jnp.float32
bf16 = jnp.bfloat16


def split3(v):
    hi = v.astype(bf16)
    rest = v - hi.astype(f32)
    mid = rest.astype(bf16)
    low = (rest - mid.astype(f32)).astype(bf16)
    return hi, mid, low


def nt(a, b):
    return lax.dot_general(a, b, (((1,), (1,)), ((), ())), preferred_element_type=f32)


def nn(a, b):
    return lax.dot_general(a, b, (((1,), (0,)), ((), ())), preferred_element_type=f32)


def local_terms(glob, local, weight, resid, tracks, h_all, x_all, sums, q_ref, k_ref):
    sums[...] = jnp.zeros_like(sums)

    def first(s, carry):
        gt_low = jnp.transpose(glob[s].astype(f32)).astype(bf16)
        t = tracks[pl.ds(s, 1), :]
        w = weight[pl.ds(s, 1), :]
        r = resid[pl.ds(s, 1), :]
        hot = lax.broadcasted_iota(jnp.int32, (TRK, PER), 0) == t
        a = local[s]
        wa = w * a
        zero = jnp.zeros((), f32)
        row = pl.ds(pl.multiple_of(s * BW, BW), BW)
        for j in range(LOC):
            spread = jnp.where(hot, wa[j : j + 1, :], zero).astype(bf16)
            h_all[row, j * TRK : (j + 1) * TRK] = nt(gt_low, spread).astype(bf16)
        terms = []
        for i in range(LOC):
            terms.append(wa[i : i + 1, :] * a)
        terms.append(wa * r)
        terms.append(jnp.zeros((12, PER), f32))
        stacked = jnp.concatenate(terms, axis=0)
        hot_low = jnp.where(hot, jnp.ones((), f32), zero).astype(bf16)
        sums[...] += nt(jnp.concatenate(split3(stacked), axis=0), hot_low)
        return carry

    lax.fori_loop(0, LAYERS, first, 0, unroll=UNROLL1)

    total = sums[0:32] + sums[32:64] + sums[64:96]
    one = jnp.ones((1, TRK), f32)
    nil = jnp.zeros((1, TRK), f32)
    rows = [
        [total[4 * i + j : 4 * i + j + 1, :] + (one if i == j else nil) for j in range(LOC)]
        for i in range(LOC)
    ]
    inv = [[one if i == j else nil for j in range(LOC)] for i in range(LOC)]
    for p in range(LOC):
        pivot = rows[p][p]
        scaled = [v / pivot for v in rows[p]]
        scaled_inv = [v / pivot for v in inv[p]]
        for o in range(LOC):
            if o != p:
                factor = rows[o][p]
                rows[o] = [u - factor * v for u, v in zip(rows[o], scaled)]
                inv[o] = [u - factor * v for u, v in zip(inv[o], scaled_inv)]
        rows[p] = scaled
        inv[p] = scaled_inv
    for i in range(LOC):
        for j in range(LOC):
            k_ref[4 * i + j : 4 * i + j + 1, :] = -inv[i][j]
    for j in range(LOC):
        q_ref[:, j * TRK : (j + 1) * TRK] = jnp.broadcast_to(
            total[16 + j : 17 + j, :].astype(bf16), (16, TRK)
        )

    def second(s, carry):
        row = pl.ds(pl.multiple_of(s * BW, BW), BW)
        h = [h_all[row, l * TRK : (l + 1) * TRK].astype(f32) for l in range(LOC)]
        for j in range(LOC):
            x = h[0] * k_ref[j : j + 1, :]
            for l in range(1, LOC):
                x = x + h[l] * k_ref[4 * l + j : 4 * l + j + 1, :]
            x_all[row, j * TRK : (j + 1) * TRK] = x.astype(bf16)
        return carry

    lax.fori_loop(0, LAYERS, second, 0, unroll=UNROLL2)


def vectors(glob, weight, resid, x_all, q_ref, v_all):
    def term(s, carry):
        wr = (weight[pl.ds(s, 1), :] * resid[pl.ds(s, 1), :]).astype(bf16)
        x = x_all[pl.ds(pl.multiple_of(s * BW, BW), BW), :]
        both = nn(jnp.broadcast_to(wr, (16, PER)), glob[s]) + nt(q_ref[...], x)
        v_all[s // 4, s % 4] = both[:8]
        return carry

    lax.fori_loop(0, LAYERS, term, 0)


def tiles_for(c, start, stop, a0, a1, a2, h_all, x_all):
    right = h_all[pl.ds(pl.multiple_of(c * 2 * BW, 2 * BW), 2 * BW), :]

    def gram(y, carry):
        out = nt(x_all[pl.ds(pl.multiple_of(y * 4 * BW, 4 * BW), 4 * BW), :], right)
        for z in range(4):
            part = out[z * BW : (z + 1) * BW, :]
            a0[y, z, c] = part[0:88, :BW]
            a1[z, c, y, 0:40] = part[88:BW, :BW]
            a1[z, c, y, 40:88] = part[0:48, BW:]
            a2[c, y, z] = part[48:BW, BW:]
        return carry

    lax.fori_loop(start, stop, gram, 0)


def diagonal(c, glob, weight, a0, a1, a2):
    def own(s):
        g = glob[s]
        return nn((jnp.transpose(g.astype(f32)) * weight[pl.ds(s, 1), :]).astype(bf16), g)

    s = 2 * c
    y, z = s // 4, s % 4
    d = own(s)
    a0[y, z, c] += d[0:88]
    a1[z, c, y, 0:40] += d[88:BW]
    d = own(s + 1)
    a1[z + 1, c, y, 40:88] += d[0:48]
    a2[c, y, z + 1] += d[48:BW]


def coords():
    r, c = lax.axis_index("row"), lax.axis_index("col")
    return {"y": r // 4, "z": r % 4, "X": c}


def moved(me, dim, offset, sign):
    if dim == "X":
        x, k = me["X"] // 2, me["X"] % 2
        dx, dk = offset // 2, offset % 2
        return ((x + 4 + sign * dx) % 4) * 2 + (k + dk) % 2
    return (me[dim] + 4 + sign * offset) % 4


def device(me, dim, place):
    at = dict(me)
    at[dim] = place
    return (at["y"] * 4 + at["z"], at["X"])


def offsets(dim):
    return WIDE if dim == "X" else RING


def greet(me, dims):
    barrier = pltpu.get_barrier_semaphore()
    count = 0
    for dim in dims:
        for o in offsets(dim):
            pl.semaphore_signal(
                barrier,
                inc=1,
                device_id=device(me, dim, moved(me, dim, o, 1)),
                device_id_type=MESH,
            )
            count += 1
    return barrier, count


def exchange_kernel(*refs):
    given, refs = refs[:5], refs[5:]
    e, v_out, b, cc = refs[0:3], refs[3], refs[4:7], refs[7:10]
    a = refs[10:13]
    bounce2 = refs[13:16]
    h_all, x_all, v_all, v_mid, sums, q_ref, k_ref = refs[16:23]
    ssem, r1, r2, r3, into_sem, out_sem, v_sem = refs[23:30]
    glob, local, weight, resid, tracks, in_sem = refs[30:36]
    loads = [
        pltpu.make_async_copy(src, dst, in_sem.at[i])
        for i, (src, dst) in enumerate(zip(given, (glob, local, weight, resid, tracks)))
    ]
    for cp in loads:
        cp.start()
    me = coords()
    barrier, count = greet(me, ("y", "z", "X"))
    for cp in loads:
        cp.wait()
    local_terms(glob, local, weight, resid, tracks, h_all, x_all, sums, q_ref, k_ref)
    pl.semaphore_wait(barrier, count)

    def send(src, dst, ssem, rsem, dim, place):
        cp = pltpu.make_async_remote_copy(
            src_ref=src,
            dst_ref=dst,
            send_sem=ssem,
            recv_sem=rsem,
            device_id=device(me, dim, place),
            device_id_type=MESH,
        )
        cp.start()

    def wait_for(ref, sem):
        pltpu.make_async_copy(ref, ref, sem).wait()

    pending = []

    def local_copy(src, mid, dst, sem):
        into = pltpu.make_async_copy(src, mid, into_sem)
        into.start()
        pending.append((into, pltpu.make_async_copy(mid, dst, sem)))

    def flush():
        for into, out in pending:
            into.wait()
            out.start()
        pending.clear()

    def stage1(j):
        o = CHUNKS[j]
        c = moved(me, "X", o, 1)
        for oo in RING:
            to = moved(me, "y", oo, 1)
            send(a[0].at[to, :, c], b[0].at[me["y"], :, c], ssem.at[0, 0], r1.at[0, oo], "y", to)
            to = moved(me, "z", oo, 1)
            send(a[1].at[to, c], b[1].at[me["z"], c], ssem.at[0, 1], r1.at[1, oo], "z", to)
        if o:
            send(a[2].at[c], b[2].at[me["X"]], ssem.at[0, 2], r1.at[2, o], "X", c)

    for j, o in enumerate(CHUNKS):
        c = moved(me, "X", o, 1)
        tiles_for(c, 0, 1, *a, h_all, x_all)
        if j:
            stage1(j - 1)
        tiles_for(c, 1, 4, *a, h_all, x_all)
        diagonal(c, glob, weight, *a)
    vectors(glob, weight, resid, x_all, q_ref, v_all)
    stage1(7)
    for oo in RING:
        to = moved(me, "y", oo, 1)
        send(v_all.at[to], v_mid.at[me["y"]], v_sem.at[0], v_sem.at[1], "y", to)
    v_mid[me["y"]] = v_all[me["y"]]

    for step in range(8):
        for g, order in enumerate(ORDERS):
            d1, d2, _ = order
            offs = (0,) + offsets(d1)
            if step >= len(offs):
                continue
            o1 = offs[step]
            src1 = moved(me, d1, o1, -1)
            if o1:
                wait_for(b[g].at[src1], r1.at[g, o1])
            for o2 in offsets(d2):
                to = moved(me, d2, o2, 1)
                src = b[g].at[src1, to] if o1 else a[g].at[me[d1], to]
                send(src, cc[g].at[me[d2], src1], ssem.at[1, g], r2.at[g, o2], d2, to)
            flush()
            back = cc[g].at[me[d2], src1]
            if o1:
                local_copy(b[g].at[src1, me[d2]], bounce2[g].at[o1], back, out_sem.at[0, g])
            else:
                pltpu.make_async_copy(a[g].at[me[d1], me[d2]], back, out_sem.at[0, g]).start()
    wait_for(v_mid.at[0:3], v_sem.at[1])
    for oo in RING:
        to = moved(me, "z", oo, 1)
        send(v_mid.at[:, to], v_out.at[me["z"]], v_sem.at[2], v_sem.at[3], "z", to)
    v_out[me["z"]] = v_mid[:, me["z"]]
    flush()
    for step in range(8):
        for g, order in enumerate(ORDERS):
            d1, d2, d3 = order
            offs = (0,) + offsets(d2)
            if step >= len(offs):
                continue
            o2 = offs[step]
            src2 = moved(me, d2, o2, -1)
            wait_for(cc[g].at[src2], r2.at[g, o2] if o2 else out_sem.at[0, g])
            for o3 in offsets(d3):
                to = moved(me, d3, o3, 1)
                send(
                    cc[g].at[src2, :, to],
                    e[g].at[me[d3], src2],
                    ssem.at[2, g],
                    r3.at[g],
                    d3,
                    to,
                )
            pltpu.make_async_copy(
                cc[g].at[src2, :, me[d3]], e[g].at[me[d3], src2], out_sem.at[1, g]
            ).start()
    wait_for(v_mid.at[0:3], v_sem.at[3])
    for g, order in enumerate(ORDERS):
        n1, n2, n3 = (SIZE[d] for d in order)
        wait_for(e[g].at[me[order[2]]], out_sem.at[1, g])
        wait_for(e[g].at[0 : n3 - 1], r3.at[g])
        wait_for(b[g].at[0 : n1 - 1], ssem.at[0, g])
        wait_for(cc[g].at[0 : n2 - 1], ssem.at[1, g])
        wait_for(e[g].at[0 : n3 - 1], ssem.at[2, g])
    wait_for(v_mid.at[0:3], v_sem.at[0])
    wait_for(v_mid.at[0:3], v_sem.at[2])


def exchange(glob, local, weight, resid, tracks):
    sizes = [tuple(SIZE[d] for d in order) for order in ORDERS]
    items = [(rows, BW) for rows in ROWS]
    both = list(zip(sizes, items))
    shapes = (
        [pltpu.VMEM((n3, n2, n1) + it, f32) for (n1, n2, n3), it in both]
        + [jax.ShapeDtypeStruct((4, 4, 8, BW), f32)]
        + [jax.ShapeDtypeStruct((n1, n2, n3) + it, f32) for (n1, n2, n3), it in both]
        + [jax.ShapeDtypeStruct((n2, n1, n3) + it, f32) for (n1, n2, n3), it in both]
    )
    any_ = pl.BlockSpec(memory_space=pl.ANY)
    vmem = pl.BlockSpec(memory_space=pltpu.VMEM)
    out = pl.pallas_call(
        exchange_kernel,
        out_shape=tuple(shapes),
        in_specs=[pl.BlockSpec(memory_space=pltpu.HBM)] * 5,
        out_specs=(vmem,) * 3 + (vmem,) + (any_,) * 6,
        scratch_shapes=[pltpu.VMEM(n + it, f32) for n, it in both]
        + [pltpu.VMEM((n1, n3) + it, f32) for (n1, n2, n3), it in both]
        + [
            pltpu.VMEM((LAYERS * BW, LOC * TRK), bf16),
            pltpu.VMEM((LAYERS * BW, LOC * TRK), bf16),
            pltpu.VMEM((4, 4, 8, BW), f32),
            pltpu.VMEM((4, 4, 8, BW), f32),
            pltpu.VMEM((96, TRK), f32),
            pltpu.VMEM((16, LOC * TRK), bf16),
            pltpu.VMEM((16, TRK), f32),
            pltpu.SemaphoreType.DMA((3, 3)),
            pltpu.SemaphoreType.DMA((3, 8)),
            pltpu.SemaphoreType.DMA((3, 8)),
            pltpu.SemaphoreType.DMA((3,)),
            pltpu.SemaphoreType.DMA,
            pltpu.SemaphoreType.DMA((2, 3)),
            pltpu.SemaphoreType.DMA((4,)),
            pltpu.VMEM(glob.shape, bf16),
            pltpu.VMEM(local.shape, f32),
            pltpu.VMEM(weight.shape, f32),
            pltpu.VMEM(resid.shape, f32),
            pltpu.VMEM(tracks.shape, jnp.int32),
            pltpu.SemaphoreType.DMA((5,)),
        ],
        compiler_params=pltpu.CompilerParams(
            collective_id=0, has_side_effects=True, vmem_limit_bytes=36 << 20
        ),
        name="exchange",
    )(glob, local, weight, resid, tracks)
    return out[:4]


def place_kernel(
    given_b, given_w, e0, e1, e2, vec, schur, product, diag, acc0, acc1, w_ref, p_ref, blocks, weak, rhs, sem, lsem
):
    row, col = lax.axis_index("row"), lax.axis_index("col")

    load_b = pltpu.make_async_copy(given_b, blocks, lsem.at[0])
    load_w = pltpu.make_async_copy(given_w, weak, lsem.at[1])
    load_b.start()
    load_w.start()
    acc0[...] = jnp.zeros_like(acc0)
    acc1[...] = jnp.zeros_like(acc1)
    rhs[...] = jnp.zeros_like(rhs)
    load_b.wait()

    def batch(xb, carry):
        def bundle(i, carry):
            y, z = i // 4, i % 4
            b = i * 8 + xb
            l0 = pl.ds(pl.multiple_of(blocks[2 * col, b] * BW, BW), BW)
            l1 = pl.ds(pl.multiple_of(blocks[2 * col + 1, b] * BW, BW), BW)
            r = pl.multiple_of(blocks[row, b] * BW, BW)
            top, low = pl.ds(r, 88), pl.ds(r + 88, 40)
            head, rest = pl.ds(r, 48), pl.ds(r + 48, 80)
            v_top = acc0[top, l0] + e0[xb, z, y]
            v_head = acc1[head, l1] + e1[y, xb, z, 40:88]
            v_low = acc0[low, l0] + e1[y, xb, z, 0:40]
            v_rest = acc1[rest, l1] + e2[z, y, xb]
            acc0[top, l0] = v_top
            acc1[head, l1] = v_head
            acc0[low, l0] = v_low
            acc1[rest, l1] = v_rest
            return carry

        return lax.fori_loop(0, 16, bundle, carry, unroll=4)

    lax.fori_loop(0, 8, batch, 0)
    load_w.wait()
    w = weak[...]
    w_hi = w.astype(bf16)
    w_ref[0:64, :] = w_hi
    w_ref[64:128, :] = (w - w_hi.astype(f32)).astype(bf16)
    p_ref[...] = jnp.zeros_like(p_ref)


    def finish_half(half, acc):
        def copy_out(ch):
            cols = pl.ds(pl.multiple_of(ch * 256, 256), 256)
            there = pl.ds(pl.multiple_of(half * GB * BW + ch * 256, 256), 256)
            return pltpu.make_async_copy(
                acc.at[:, cols], schur.at[:, there], sem.at[half * 4 + ch]
            )

        owner = (row % 2 == half) & (col == row // 2)

        @pl.when(jnp.logical_not(owner))
        def _():
            for ch in range(4):
                copy_out(ch).start()

        def chunk(ch, carry):
            cols = pl.ds(pl.multiple_of(ch * 256, 256), 256)
            wc = w_ref[:, pl.ds(pl.multiple_of(half * GB * BW + ch * 256, 256), 256)]
            v = acc[:, cols]
            hi = v.astype(bf16)
            lo = (v - hi.astype(f32)).astype(bf16)
            p_ref[...] += nt(hi, wc) + nt(lo, wc)

            @pl.when(row % 2 == half)
            def _():
                for m in range(2):
                    k = 2 * ch + m
                    at = pl.ds(pl.multiple_of(k * BW, BW), BW)
                    diag[k // 2, m] = acc[at, at]

            @pl.when(owner)
            def _():
                acc[:, cols] = jnp.zeros((GB * BW, 256), f32)
                copy_out(ch).start()

            return carry

        lax.fori_loop(0, 4, chunk, 0)
        return copy_out

    outs = [finish_half(0, acc0), finish_half(1, acc1)]

    def term(i, carry):
        k = blocks[row, i * 8 + col]
        rhs[pl.ds(k, 1), :] += vec[i % 4, i // 4, 0:1]
        return carry

    lax.fori_loop(0, 16, term, 0)
    for k in range(GB):
        pt = jnp.transpose(p_ref[k * BW : (k + 1) * BW, :])
        product[k // 2, k % 2, 0:64] = pt[0:64] + pt[64:128]
        product[k // 2, k % 2, 64:72] = rhs[...]
    for copy_out in outs:
        for ch in range(4):
            copy_out(ch).wait()


def place(blocks, weak, e0, e1, e2, vec):
    vmem = pl.BlockSpec(memory_space=pltpu.VMEM)
    any_ = pl.BlockSpec(memory_space=pl.ANY)
    hbm = pl.BlockSpec(memory_space=pltpu.HBM)
    return pl.pallas_call(
        place_kernel,
        in_specs=[hbm, hbm, vmem, vmem, vmem, vmem],
        out_specs=(any_, vmem, vmem),
        out_shape=(
            jax.ShapeDtypeStruct((GB * BW, 2 * GB * BW), f32),
            jax.ShapeDtypeStruct((4, 2, 72, BW), f32),
            jax.ShapeDtypeStruct((4, 2, BW, BW), f32),
        ),
        scratch_shapes=[
            pltpu.VMEM((GB * BW, GB * BW), f32),
            pltpu.VMEM((GB * BW, GB * BW), f32),
            pltpu.VMEM((BW, 2 * GB * BW), bf16),
            pltpu.VMEM((GB * BW, BW), f32),
            pltpu.SMEM(blocks.shape, jnp.int32),
            pltpu.VMEM(weak.shape, f32),
            pltpu.VMEM((GB, BW), f32),
            pltpu.SemaphoreType.DMA((8,)),
            pltpu.SemaphoreType.DMA((2,)),
        ],
        compiler_params=pltpu.CompilerParams(vmem_limit_bytes=20 << 20),
        name="place",
    )(blocks, weak, e0, e1, e2, vec)


def finish_kernel(product, diag, weak, tile, rhs, near, chip, far, spare, ssem, rsem):
    me = coords()
    row = lax.axis_index("row")
    mine = me["X"]
    x, k = mine // 2, mine % 2
    owner = row // 2
    barrier, count = greet(me, ("X",))
    pl.semaphore_wait(barrier, count)

    def copy(src, dst, i, to):
        return pltpu.make_async_remote_copy(
            src_ref=src,
            dst_ref=dst,
            send_sem=ssem.at[i],
            recv_sem=rsem.at[i],
            device_id=device(me, "X", to),
            device_id_type=MESH,
        )

    def wait_for(ref, sem):
        pltpu.make_async_copy(ref, ref, sem).wait()

    copy(product.at[:, 1 - k], near, 0, moved(me, "X", 1, 1)).start()

    @pl.when(mine == owner)
    def _():
        for o in WIDE:
            to = moved(me, "X", o, 1)
            copy(diag.at[to // 2, to % 2], tile, 2, to).start()
        tile[...] = diag[x, k]

    wait_for(near, rsem.at[0])
    for i in range(4):
        chip[i] = product[i, k] + near[i]
    wait_for(near, ssem.at[0])
    for dx in (2, 1, 3):
        to = moved(me, "X", 2 * dx, 1)
        copy(chip.at[to // 2], far.at[dx - 1], 1, to).start()
    total = chip[x]
    wait_for(far, rsem.at[1])
    total = total + far[0] + far[1] + far[2]
    weak[...] = total[0:64]
    rhs[...] = total[64:72]
    wait_for(far, ssem.at[1])

    @pl.when(mine != owner)
    def _():
        wait_for(tile, rsem.at[2])

    @pl.when(mine == owner)
    def _():
        wait_for(spare, ssem.at[2])


def finish(product, diag):
    vmem = pl.BlockSpec(memory_space=pltpu.VMEM)
    return pl.pallas_call(
        finish_kernel,
        out_shape=(
            jax.ShapeDtypeStruct((64, BW), f32),
            jax.ShapeDtypeStruct((BW, BW), f32),
            jax.ShapeDtypeStruct((GB, BW), f32),
        ),
        in_specs=[vmem] * 2,
        out_specs=(vmem,) * 3,
        scratch_shapes=[
            pltpu.VMEM((4, 72, BW), f32),
            pltpu.VMEM((4, 72, BW), f32),
            pltpu.VMEM((3, 72, BW), f32),
            pltpu.VMEM((7, BW, BW), f32),
            pltpu.SemaphoreType.DMA((3,)),
            pltpu.SemaphoreType.DMA((3,)),
        ],
        compiler_params=pltpu.CompilerParams(
            collective_id=1, has_side_effects=True, vmem_limit_bytes=8 << 20
        ),
        name="finish",
    )(product, diag)


def emit_kernel(weak_in, tile, rhs_in, weak, layer, rhs):
    col = lax.axis_index("col")
    weak[...] = weak_in[...]
    rhs[...] = rhs_in[...]
    layer[...] = jnp.zeros_like(layer)
    layer[pl.ds(pl.multiple_of(col * BW, BW), BW), :] = tile[...]


def emit(weak, tile, rhs):
    vmem = pl.BlockSpec(memory_space=pltpu.VMEM)
    return pl.pallas_call(
        emit_kernel,
        out_shape=(
            jax.ShapeDtypeStruct((64, BW), f32),
            jax.ShapeDtypeStruct((GB * BW, BW), f32),
            jax.ShapeDtypeStruct((GB, BW), f32),
        ),
        in_specs=[vmem] * 3,
        out_specs=(vmem,) * 3,
        compiler_params=pltpu.CompilerParams(vmem_limit_bytes=8 << 20),
        name="emit",
    )(weak, tile, rhs)


def body(glob_derivs, local_derivs, weights, residuals, track_ids, module_blocks, weak_modes):
    def stay(v):
        return pltpu.with_memory_space_constraint(v, pltpu.HBM)

    inputs = (glob_derivs, local_derivs, weights, residuals, track_ids)
    e = exchange(*[stay(v[0]) for v in inputs])
    schur, product, diag = place(stay(module_blocks.T), stay(weak_modes.T), *e)
    weak, layer, rhs = emit(*finish(product, diag))
    return schur, layer, rhs.reshape(GB * BW), weak.T


def solution(mesh):
    placed = (
        P(("row", "col"), None, None, None),
        P(("row", "col"), None, None, None),
        P(("row", "col"), None, None),
        P(("row", "col"), None, None),
        P(("row", "col"), None, None),
        P(),
        P("col", None),
    )
    return jax.shard_map(
        body,
        mesh=mesh,
        in_specs=placed,
        out_specs=(P("row", "col"), P("row", "col"), P("row"), P(("row", "col"), None)),
        check_vma=False,
    )
```
